32 devices in a mesh: dp: 4 (over z), seq: 4 (over x, core), mp: 2 (over y).
Axes of the slice: x: 2, y: 2, z: 4, core: 2. Of those that a mesh axis runs over, the one named last changes fastest.
Arguments:
- queries: bfloat16 [2048, 4096], P(('dp', 'seq'), 'mp'), may hold values from -2 to 2
- key_rows: bfloat16 [2048, 4096], P(('dp', 'seq'), 'mp'), may hold values from -2 to 2
- value_rows: bfloat16 [2048, 4096], P(('dp', 'seq'), 'mp'), may hold values from -6 to 6
- row_plan: int32 [4, 4], replicated, may hold values from 0 to 40, as said below
- segments: int32 [4, 512], P('dp', 'seq'), may hold values from 0 to 5, never falling along the last dimension, each value on 1 to 256 neighbouring positions
- norm_gain: float32 [4096], P('mp'), may hold values from 0.5 to 1.5
- out_weight: bfloat16 [4096, 3072], P('mp'), may hold values from -0.09375 to 0.09375
- out_grad: bfloat16 [2048, 3072], P(('dp', 'seq'), 'mp'), may hold values from -6 to 6
Outputs:
- normed: bfloat16 [2048, 4096], P(('dp', 'seq'), 'mp')
- query_grad: bfloat16 [2048, 4096], P(('dp', 'seq'), 'mp')
- key_grad: bfloat16 [2048, 4096], P(('dp', 'seq'), 'mp')
- value_grad: bfloat16 [2048, 4096], P(('dp', 'seq'), 'mp')
- weight_grad: float32 [3072, 4096], P(('dp', 'seq'), 'mp')
The draws below stay inside these ranges and needn't reach their ends.
Inputs may be any that keep to these rules, and one draw needn't show every extreme that they name: Each row and each column of row_plan sums to 128; the plan holds for every sequence shard alike; an arriving group's rows for group 0 come first, then those for group 1, and so on. `segments`: documents never cross data groups.
All inputs are finite; a program needn't handle non-finite values.
Results may differ from the reference program's by a relative error of at most 0.0064.
Values may be sent and summed in bfloat16 or wider, within the bound.
A program may use at most 128 MiB of HBM per device.

```python
import math
import jax
import jax.numpy as jnp
import numpy as np
from jax import lax

HS = 128
HL = 32
DOUT = 3072
ROWS = 128
COUNT = 6
HISTORY = 512
MOST = 256
CAP = 40
TOKENS = 2048
N_DP = 4
N_SEQ = 4


def draw_row_plan(key, part):
    first_key, second_key, third_key, fourth_key = jax.random.split(jax.random.fold_in(key, 17), 4)
    remaining = ROWS - CAP
    shuffled = jax.random.permutation(first_key, (N_DP - 1) * CAP)
    taken = (jnp.arange((N_DP - 1) * CAP) < remaining).astype(jnp.int32)
    bin_index = shuffled // CAP
    rest_weights = jnp.zeros((N_DP - 1,), jnp.int32).at[bin_index].add(taken)
    weights = jnp.concatenate([jnp.full((1,), CAP, jnp.int32), rest_weights])
    weights = weights[jax.random.permutation(second_key, N_DP)]
    source_perm = jax.random.permutation(third_key, N_DP)
    target_perm = jax.random.permutation(fourth_key, N_DP)
    offsets = (target_perm[None, :] - source_perm[:, None]) % N_DP
    return weights[offsets].astype(jnp.int32)


def with_spikes(result, stream_key, source, target, blocks, factor):
    owner, partner = [(jnp.arange(result.shape[position]) // (result.shape[position] // blocks)).reshape([-1 if axis == position else 1 for axis in range(result.ndim)]) for position in (source, target)]
    chosen = jax.random.permutation(stream_key, blocks)[partner]
    strong = (owner == chosen) | (owner == (partner + blocks // 2) % blocks)
    return jnp.where(strong, factor * result, result)


def block_levels(rng, dims, shards, smallest, largest):
    level = 1.0
    for axis_at, shards_of in shards:
        draws = jax.random.uniform(jax.random.fold_in(jax.random.fold_in(rng, 6), axis_at), (shards_of,), jnp.float32, smallest / len(shards), largest / len(shards))
        level = level * jnp.repeat(jnp.exp(draws), dims[axis_at] // shards_of).reshape((-1,) + (1,) * (len(dims) - 1 - axis_at))
    return level


def length_profile(count, total, reach, lean):
    loads = [(1 << 20) // math.isqrt(rank ** lean) + 1 for rank in range(2, count + 1)]
    surplus, given = total - reach - (count - 1), [1] * (count - 1)
    while surplus > 0:
        candidates = [i for i in range(count - 1) if given[i] < reach]
        mass, left = sum([loads[i] for i in candidates]), surplus
        for i in candidates:
            more = min(reach - given[i], max(1, left * loads[i] // mass), surplus)
            given[i] = given[i] + more
            surplus = surplus - more
    return np.array([reach] + given)


def ragged_sizes(key, count, total, most, skew):
    if count == 2:
        one = jax.random.randint(key, (), max(1, total - most), min(most, total - 1) + 1)
        return jnp.stack([one, total - one])
    sizes = jnp.asarray(length_profile(count, total, most, skew), jnp.int32)
    couples = (count - 1) // 2
    giver, receiver = sizes[1:1 + 2 * couples:2], sizes[2:2 + 2 * couples:2]
    room = jnp.minimum(giver - 1, most - receiver)
    moved = jax.random.randint(jax.random.fold_in(key, 1), (couples,), 0, 1 << 20) % (room + 1)
    sizes = sizes.at[1:1 + 2 * couples:2].set(giver - moved).at[2:2 + 2 * couples:2].set(receiver + moved)
    return sizes[jax.random.permutation(jax.random.fold_in(key, 2), count)]


def scatter_about(rng, shape, spread, most, cuts=(), kind=jnp.bfloat16):
    entries = jax.random.normal(rng, shape, jnp.float32) * spread
    if len(cuts) > 0:
        entries = block_levels(rng, shape, cuts, -0.22, 0.18) * entries
    return jnp.clip(entries, min=-most, max=most).astype(kind)


def noise_with(key, shape, spread, bound, shards, heavy, kind=jnp.bfloat16):
    result = spread * jax.random.normal(key, shape, jnp.float32)
    if shards:
        result = result * block_levels(key, shape, shards, -0.22, 0.18)
    return jnp.clip(with_spikes(result, jax.random.fold_in(key, 3), *heavy), -bound, bound).astype(kind)


def setup_inputs(seed: int = 0) -> dict:
    arg_keys = jax.random.split(jax.random.key(seed), 9)
    queries = scatter_about(arg_keys[0], (TOKENS, HL * HS), 0.3, 2.0, ((0, 16), (1, 2)))
    key_rows = scatter_about(arg_keys[1], (TOKENS, HL * HS), 0.3, 2.0, ((0, 16), (1, 2)))
    value_rows = scatter_about(arg_keys[2], (TOKENS, HL * HS), 1.0, 6.0, ((0, 16), (1, 2)))
    row_plan = draw_row_plan(jax.random.fold_in(arg_keys[8], 71), 0)
    segments = jax.vmap(lambda own: jnp.searchsorted(jnp.cumsum(ragged_sizes(own, COUNT, HISTORY, MOST, 2)), jnp.arange(HISTORY), side="right"))(jax.random.split(arg_keys[4], N_DP)).reshape((N_DP, HISTORY)).astype(jnp.int32)
    norm_gain = jnp.clip(0.5 + 1.0 * jax.random.uniform(arg_keys[5], (HL * HS,), jnp.float32) ** block_levels(arg_keys[5], (HL * HS,), ((0, 2),), -0.2, 0.2), 0.5, 1.5)
    out_weight = scatter_about(arg_keys[6], (HL * HS, DOUT), (HL * HS) ** -0.5, 0.09375, ((0, 2),))
    out_grad = noise_with(arg_keys[7], (TOKENS, DOUT), 1.0, 6.0, ((0, 16), (1, 2)), (0, 1, 16, 2.0))
    return dict(queries=queries, key_rows=key_rows, value_rows=value_rows, row_plan=row_plan, segments=segments, norm_gain=norm_gain, out_weight=out_weight, out_grad=out_grad)


NORM_EPS = 1e-06
HIGH = lax.Precision.HIGHEST

def to_half(values):
    return lax.optimization_barrier(values.astype(jnp.bfloat16)).astype(jnp.float32)

def rms_scale(attn, gain_heads):
    power = lax.optimization_barrier(jnp.mean(attn * attn, axis=-1, keepdims=True))
    return attn * lax.rsqrt(power + NORM_EPS) * gain_heads

def route_index(row_plan):
    send_start = jnp.cumsum(row_plan, axis=1) - row_plan
    recv_start = jnp.cumsum(row_plan, axis=0) - row_plan
    recv_end = recv_start + row_plan
    positions = jnp.arange(ROWS, dtype=jnp.int32)
    source = lax.optimization_barrier(jnp.sum((recv_end.T[:, None, :] <= positions[None, :, None]).astype(jnp.int32), axis=2)).astype(jnp.int32)
    target = jnp.arange(N_DP, dtype=jnp.int32)[:, None]
    offset = positions[None, :] - recv_start[source, target] + send_start[source, target]
    return (source, offset.astype(jnp.int32))

def doc_mask(seg_block):
    positions = jnp.arange(seg_block.shape[0], dtype=jnp.int32)
    causal = positions[None, :] <= positions[:, None]
    return (causal & (seg_block[:, None] == seg_block[None, :])).astype(jnp.float32)

def block_forward(carry, block):
    state, last_id = carry
    query, keyv, value, seg_f = block
    same_doc = doc_mask(seg_f)
    scores = to_half(jnp.einsum('thd,shd->hts', query, keyv, precision=HIGH) * same_doc[None])
    inner = jnp.einsum('hts,she->the', scores, value, precision=HIGH)
    carried = (seg_f == last_id).astype(jnp.float32)
    outer = jnp.einsum('thd,hde->the', query, state, precision=HIGH) * carried[:, None, None]
    tail = (seg_f == seg_f[-1]).astype(jnp.float32)
    local_state = jnp.einsum('thd,the->hde', keyv * tail[:, None, None], value, precision=HIGH)
    new_state = local_state + jnp.where(seg_f[-1] == last_id, state, jnp.zeros_like(state))
    return ((new_state, seg_f[-1]), (inner + outer, state, last_id))

def block_backward(carry, block):
    rstate, first_id = carry
    query, keyv, value, seg_f, d_attn, fstate, fid = block
    same_doc = doc_mask(seg_f)
    d_round = to_half(d_attn)
    scores = to_half(jnp.einsum('thd,shd->hts', query, keyv, precision=HIGH) * same_doc[None])
    dprob = to_half(jnp.einsum('the,she->hts', d_round, value, precision=HIGH) * same_doc[None])
    carried = (seg_f == fid).astype(jnp.float32)
    rev_use = (seg_f == first_id).astype(jnp.float32)
    dquery = jnp.einsum('hts,shd->thd', dprob, keyv, precision=HIGH)
    dquery = dquery + jnp.einsum('the,hde->thd', d_attn, fstate, precision=HIGH) * carried[:, None, None]
    dkey = jnp.einsum('hts,thd->shd', dprob, query, precision=HIGH)
    dkey = dkey + jnp.einsum('the,hde->thd', value, rstate, precision=HIGH) * rev_use[:, None, None]
    dvalue = jnp.einsum('hts,the->she', scores, d_round, precision=HIGH)
    dvalue = dvalue + jnp.einsum('thd,hde->the', keyv, rstate, precision=HIGH) * rev_use[:, None, None]
    head_part = (seg_f == seg_f[0]).astype(jnp.float32)
    local_r = jnp.einsum('thd,the->hde', query * head_part[:, None, None], d_attn, precision=HIGH)
    new_r = local_r + jnp.where(seg_f[0] == first_id, rstate, jnp.zeros_like(rstate))
    return ((new_r, seg_f[0]), (dquery, dkey, dvalue))

def reference(queries, key_rows, value_rows, row_plan, segments, norm_gain, out_weight, out_grad):
    width = queries.shape[1]
    heads = width // HS
    source, offset = route_index(row_plan)
    shard_ids = jnp.arange(N_SEQ, dtype=jnp.int32)[None, :, None]

    def reorder(whole):
        split = whole.reshape(N_DP, N_SEQ, ROWS, width)
        return split[source[:, None, :], shard_ids, offset[:, None, :]].reshape(N_DP, N_SEQ * ROWS, width)
    q_all = reorder(queries)
    k_all = reorder(key_rows)
    v_all = reorder(value_rows)
    grad_all = out_grad.reshape(N_DP, N_SEQ * ROWS, DOUT)
    gain_heads = norm_gain.reshape(heads, HS)
    length = N_SEQ * ROWS

    def one_group(weight_acc, group):
        query_g, key_g, value_g, seg_g, grad_g = group
        query = query_g.astype(jnp.float32).reshape(N_SEQ, ROWS, heads, HS)
        keyv = key_g.astype(jnp.float32).reshape(N_SEQ, ROWS, heads, HS)
        value = value_g.astype(jnp.float32).reshape(N_SEQ, ROWS, heads, HS)
        seg_f = seg_g.astype(jnp.float32).reshape(N_SEQ, ROWS)
        start = (jnp.zeros((heads, HS, HS), jnp.float32), jnp.full((), -1.0, jnp.float32))
        _, (attn, fstate, fid) = lax.scan(block_forward, start, (query, keyv, value, seg_f))
        attn_flat = attn.reshape(length, heads, HS)
        normed_f, pull = jax.vjp(lambda a: rms_scale(a, gain_heads), attn_flat)
        normed = normed_f.reshape(length, width).astype(jnp.bfloat16)
        d_normed = lax.dot_general(grad_g, out_weight, (((1,), (1,)), ((), ())), preferred_element_type=jnp.float32)
        d_attn = pull(d_normed.reshape(length, heads, HS))[0]
        d_blocks = d_attn.reshape(N_SEQ, ROWS, heads, HS)
        _, (dquery, dkey, dvalue) = lax.scan(block_backward, start, (query, keyv, value, seg_f, d_blocks, fstate, fid), reverse=True)
        term = lax.dot_general(grad_g, normed, (((0,), (0,)), ((), ())), preferred_element_type=jnp.float32)
        results = (normed, dquery.reshape(length, width).astype(jnp.bfloat16), dkey.reshape(length, width).astype(jnp.bfloat16), dvalue.reshape(length, width).astype(jnp.bfloat16))
        return (weight_acc + term, results)
    weight_grad, (normed, query_grad, key_grad, value_grad) = lax.scan(one_group, jnp.zeros((DOUT, width), jnp.float32), (q_all, k_all, v_all, segments, grad_all))
    total = N_DP * length
    return (normed.reshape(total, width), query_grad.reshape(total, width), key_grad.reshape(total, width), value_grad.reshape(total, width), weight_grad)
```

```python
import functools

import jax
import jax.numpy as jnp
from jax import lax
from jax.experimental import pallas as pl
from jax.experimental.pallas import tpu as pltpu
from jax.sharding import PartitionSpec as P

HS = 128
NORM_EPS = 1e-06
F32 = jnp.float32
BF16 = jnp.bfloat16
MESH = pl.DeviceIdType.MESH
K, V, Q = 0, 1, 2


def mm(a, b, ca, cb):
    return lax.dot_general(a, b, (((ca,), (cb,)), ((), ())), preferred_element_type=F32)


def plan_sizes(mesh, rows, width, out_half):
    groups, shards, splits = mesh.shape["dp"], mesh.shape["seq"], mesh.shape["mp"]
    z = {}
    z["D"], z["S"], z["M"], z["X"] = groups, shards, splits, shards // 2
    z["R"], z["W"], z["DM"] = rows, width, out_half
    z["DOUT"] = out_half * splits
    heads = width // HS
    z["HC"] = 4 if heads % 4 == 0 else 1
    z["NC"] = heads // z["HC"]
    z["CW"] = z["HC"] * HS
    z["CAP"] = rows // min(groups, 8) + rows // 16
    z["CP"] = -(-z["CAP"] // 16) * 16
    z["RB"] = z["DOUT"] // (groups * shards)
    z["PX"] = splits // z["X"]
    z["RP"] = z["RB"] // z["PX"]
    return z


def scratch_of(z):
    D, M, X, R, W, NC, CW = (z[n] for n in ("D", "M", "X", "R", "W", "NC", "CW"))
    XO = max(1, X - 1)
    vm = pltpu.VMEM
    dma = pltpu.SemaphoreType.DMA
    return dict(
        x=vm((3, R, W), BF16),
        snd=vm((3, NC, D, z["CP"], CW), BF16),
        arr=vm((3, NC, D, z["CP"], CW), BF16),
        f=vm((3, NC, R, CW), BF16),
        w=vm((NC, CW, z["DOUT"]), BF16),
        g=vm((M, R, z["DM"]), BF16),
        gt=vm((z["DOUT"], R), BF16),
        gz=vm((D, 2, X, z["RB"], R), BF16),
        lhs=vm((X, z["RB"], D * 2 * R), BF16),
        dn=vm((NC, R, CW), F32),
        pm=vm((NC, R, CW), BF16),
        lf=vm((HS, CW), F32),
        ls=vm((NC, HS, CW), BF16),
        st=vm((NC, HS, CW), BF16),
        rf=vm((NC, HS, CW), F32),
        lr=vm((NC, HS, CW), BF16),
        rst=vm((NC, HS, CW), BF16),
        dh=vm((NC, R, CW), BF16),
        nb=vm((NC, D, 2, R, CW), BF16),
        do=vm((3, NC, R, CW), BF16),
        acc=vm((NC, z["RB"], CW), F32),
        xs=vm((NC, XO, z["RB"], CW), BF16),
        xr=vm((NC, XO, z["RB"], CW), BF16),
        seg=vm((3, 8, R), F32),
        doc=vm((R, R), F32),
        mk=vm((4, R, R), BF16),
        jn=vm((2, 8, R), F32),
        sel=vm((D * z["CP"], R), BF16),
        pick=vm((R, D * z["CP"]), BF16),
        in_s=dma((4,)),
        w_s=dma((NC,)),
        y_ss=dma((max(1, M - 1),)),
        y_rs=dma((max(1, M - 1),)),
        sg_ss=dma((2,)),
        sg_rs=dma((2,)),
        r_ss=dma((3, NC, D)),
        r_rs=dma((3, NC, D)),
        g_ss=dma((2 * D,)),
        g_rs=dma((2 * D,)),
        b_ss=dma((max(1, M - 1),)),
        b_rs=dma((max(1, M - 1),)),
        f_ss=dma((NC,)),
        f_rs=dma((NC,)),
        v_ss=dma((NC,)),
        v_rs=dma((NC,)),
        nr_ss=dma((NC, D)),
        nl_ss=dma((NC, D)),
        n_rs=dma((NC, D)),
        p_ss=dma((NC, D)),
        p_rs=dma((NC, D)),
        x_ss=dma((NC, XO)),
        x_rs=dma((NC, XO)),
        o_s=dma((5, NC)),
    )


TAIL, HEAD, CAR, REV = 0, 1, 2, 3


def whole_body(z, names, *refs):
    plan, seg_in, gain, q_in, k_in, v_in, w_in, g_in = refs[:8]
    normed_out, dq_out, dk_out, dv_out, wg_out = refs[8:13]
    b = dict(zip(names, refs[13:]))
    D, S, M, X, R, NC, CW, HC = (z[n] for n in ("D", "S", "M", "X", "R", "NC", "CW", "HC"))
    CAP, CP, RB, RP, PX, DM = (z[n] for n in ("CAP", "CP", "RB", "RP", "PX", "DM"))
    d, s, m = lax.axis_index("dp"), lax.axis_index("seq"), lax.axis_index("mp")
    xi, co = s // 2, s % 2
    sent = []

    def remote(src, dst, ss, rs, **where):
        return pltpu.make_async_remote_copy(
            src_ref=src, dst_ref=dst, send_sem=ss, recv_sem=rs, device_id=where, device_id_type=MESH
        )

    def when(cond, act):
        if cond is None:
            act()
        else:
            pl.when(cond)(act)

    def go(copy, cond=None):
        when(cond, copy.start)
        sent.append((cond, copy))

    sources = ((k_in, b["x"].at[K]), (v_in, b["x"].at[V]), (q_in, b["x"].at[Q]), (g_in, b["g"].at[m]))
    loads = [pltpu.make_async_copy(a, c, b["in_s"].at[i]) for i, (a, c) in enumerate(sources)]
    for i in (0, 3, 1, 2):
        loads[i].start()
    w_loads = [
        pltpu.make_async_copy(w_in.at[pl.ds(c * CW, CW), :], b["w"].at[c], b["w_s"].at[c])
        for c in range(NC)
    ]

    own_seg = seg_in[...].astype(F32)
    b["seg"][0] = jnp.broadcast_to(own_seg, (8, R))
    if CP > CAP:
        b["arr"][:, :, :, CAP:CP, :] = jnp.zeros((3, NC, D, CP - CAP, CW), BF16)

    @pl.when(s == 0)
    def _():
        b["seg"][1] = jnp.full((8, R), -1.0, F32)
        b["st"][...] = jnp.zeros_like(b["st"])

    @pl.when(s == S - 1)
    def _():
        b["seg"][2] = jnp.full((8, R), -1.0, F32)
        b["rst"][...] = jnp.zeros_like(b["rst"])

    barrier = pltpu.get_barrier_semaphore()
    peers = 0

    def greet(**where):
        pl.semaphore_signal(barrier, inc=1, device_id=where, device_id_type=MESH)

    for t in range(D):
        for cc in range(2):
            if t or cc:
                greet(dp=lax.rem(d + t, D), seq=xi * 2 + (co + cc) % 2, mp=m)
                peers += 1
    for t in range(1, X):
        for cc in range(2):
            greet(dp=d, seq=lax.rem(xi + t, X) * 2 + cc, mp=m)
            peers += 1
    for t in range(1, M):
        greet(dp=d, seq=s, mp=lax.rem(m + t, M))
        peers += 1

    slot = lax.broadcasted_iota(jnp.int32, (D * CP, R), 0)
    row = lax.broadcasted_iota(jnp.int32, (D * CP, R), 1)
    start = jnp.int32(0)
    hot = jnp.zeros((D * CP, R), F32)
    for j in range(D):
        inside = (slot >= j * CP) & (slot < j * CP + CAP) & (row - start == slot - j * CP)
        hot = jnp.where(inside, 1.0, hot)
        start = start + plan[d, j]
    b["sel"][...] = hot.astype(BF16)
    slot = lax.broadcasted_iota(jnp.int32, (R, D * CP), 1)
    row = lax.broadcasted_iota(jnp.int32, (R, D * CP), 0)
    start = jnp.int32(0)
    hot = jnp.zeros((R, D * CP), F32)
    for i in range(D):
        count = plan[i, d]
        at = slot - i * CP
        inside = (at >= 0) & (at < CP) & (at == row - start) & (row - start < count)
        hot = jnp.where(inside, 1.0, hot)
        start = start + count
    b["pick"][...] = hot.astype(BF16)

    pl.semaphore_wait(barrier, peers)

    loads[3].wait()
    y_copies = []
    for t in range(1, M):
        c = remote(
            b["g"].at[m], b["g"].at[m], b["y_ss"].at[t - 1], b["y_rs"].at[t - 1], mp=lax.rem(m + t, M)
        )
        go(c)
        y_copies.append(c)
    after = remote(b["seg"].at[0], b["seg"].at[1], b["sg_ss"].at[0], b["sg_rs"].at[0], seq=lax.rem(s + 1, S))
    before = remote(
        b["seg"].at[0], b["seg"].at[2], b["sg_ss"].at[1], b["sg_rs"].at[1], seq=lax.rem(s + S - 1, S)
    )
    go(after, s < S - 1)
    go(before, s > 0)

    r_copies = {}

    def hand(a, c):
        packed = mm(b["sel"][...], b["x"][a, :, c * CW : (c + 1) * CW], 1, 0).astype(BF16)
        b["snd"][a, c] = packed.reshape(D, CP, CW)
        for t in range(1, D):
            to = lax.rem(d + t, D)
            copy = remote(
                b["snd"].at[a, c, to, pl.ds(0, CAP)],
                b["arr"].at[a, c, d, pl.ds(0, CAP)],
                b["r_ss"].at[a, c, t],
                b["r_rs"].at[a, c, t],
                dp=to,
            )
            go(copy)
            r_copies[a, c, t] = copy
        b["arr"][a, c, d] = b["snd"][a, c, d]

    loads[0].wait()
    loads[1].wait()
    for c in range(NC):
        hand(K, c)
        hand(V, c)
    for c in range(NC):
        w_loads[c].start()
    loads[2].wait()
    for c in range(NC):
        hand(Q, c)

    pl.when(s > 0)(after.wait_recv)
    pl.when(s < S - 1)(before.wait_recv)
    across = jnp.broadcast_to(b["seg"][0][0:1, :], (R, R))
    down = jnp.transpose(across)
    t_at = lax.broadcasted_iota(jnp.int32, (R, R), 0)
    u_at = lax.broadcasted_iota(jnp.int32, (R, R), 1)
    b["doc"][...] = jnp.where((u_at <= t_at) & (across == down), 1.0, 0.0)
    own_last = b["seg"][0][0:1, R - 1 : R]
    own_first = b["seg"][0][0:1, 0:1]
    last_before = b["seg"][1][0:1, R - 1 : R]
    first_after = b["seg"][2][0:1, 0:1]
    for i, value in ((TAIL, own_last), (HEAD, own_first), (CAR, last_before), (REV, first_after)):
        b["mk"][i] = jnp.where(down == jnp.broadcast_to(value, (R, R)), 1.0, 0.0).astype(BF16)
    for i, (one, two) in enumerate(((own_last, last_before), (own_first, first_after))):
        b["jn"][i] = jnp.broadcast_to(jnp.where(one == two, 1.0, 0.0), (8, R))

    for c in y_copies:
        c.wait_recv()
    for i in range(M):
        for j in range(DM // HS):
            b["gt"][pl.ds(i * DM + j * HS, HS), :] = jnp.transpose(b["g"][i, :, j * HS : (j + 1) * HS])
    px, off = m // PX, pl.multiple_of((m % PX) * RP, RP)
    g_copies = []
    for t in range(D):
        for cc in range(2):
            to, core = lax.rem(d + t, D), (co + cc) % 2
            at = pl.multiple_of(((to * X + px) * 2 + core) * RB + off, RP)
            if t == 0 and cc == 0:
                b["gz"][d, co, px, pl.ds(off, RP), :] = b["gt"][pl.ds(at, RP), :]
                continue
            copy = remote(
                b["gt"].at[pl.ds(at, RP), :],
                b["gz"].at[d, co, px, pl.ds(off, RP), :],
                b["g_ss"].at[t * 2 + cc],
                b["g_rs"].at[t * 2 + cc],
                dp=to,
                seq=xi * 2 + core,
            )
            go(copy)
            g_copies.append(copy)

    for c in range(NC):
        w_loads[c].wait()

    def grow(c, carry):
        total = mm(b["g"][0], b["w"][c, :, 0:DM], 1, 1)
        for i in range(1, M):
            total = total + mm(b["g"][i], b["w"][c, :, i * DM : (i + 1) * DM], 1, 1)
        b["dn"][c] = total
        return carry

    lax.fori_loop(0, NC, grow, 0)

    def place(a, c):
        for t in range(1, D):
            r_copies[a, c, t].wait_recv()
        parts = b["arr"][a, c].reshape(D * CP, CW)
        b["f"][a, c] = mm(b["pick"][...], parts, 1, 0).astype(BF16)

    for c in range(NC):
        place(K, c)
        place(V, c)
        for h in range(HC):
            cols = slice(h * HS, (h + 1) * HS)
            b["lf"][:, cols] = mm(b["f"][K, c, :, cols] * b["mk"][TAIL], b["f"][V, c, :, cols], 0, 0)
        copy = remote(
            b["ls"].at[c], b["st"].at[c], b["f_ss"].at[c], b["f_rs"].at[c], seq=lax.rem(s + 1, S)
        )
        pl.when(s > 0)(copy.wait_recv)
        join = jnp.broadcast_to(b["jn"][0][0:1, 0:1], (HS, CW))
        b["ls"][c] = (b["lf"][...] + jnp.where(join > 0.5, b["st"][c].astype(F32), 0.0)).astype(BF16)
        go(copy, s < S - 1)

    for copy in g_copies:
        copy.wait_recv()
    b_copies = []
    part = b["gz"].at[:, :, px, pl.ds(off, RP), :]
    for t in range(1, M):
        copy = remote(part, part, b["b_ss"].at[t - 1], b["b_rs"].at[t - 1], mp=lax.rem(m + t, M))
        go(copy)
        b_copies.append(copy)

    v_copies = []
    outs = []

    def write(index, c, src, out):
        copy = pltpu.make_async_copy(src, out.at[:, pl.ds(c * CW, CW)], b["o_s"].at[index, c])
        copy.start()
        outs.append(copy)

    def spread(c, origin, right, left):
        block = b["nb"].at[c, origin, co]
        if right is not None:
            go(remote(block, block, b["nr_ss"].at[c, origin], b["n_rs"].at[c, origin], dp=jnp.minimum(d + 1, D - 1)), right)
        if left is not None:
            go(remote(block, block, b["nl_ss"].at[c, origin], b["n_rs"].at[c, origin], dp=jnp.maximum(d - 1, 0)), left)

    def share(c, origin, cond):
        block = b["nb"].at[c, origin, co]
        go(remote(block, block, b["p_ss"].at[c, origin], b["p_rs"].at[c, origin], seq=xi * 2 + 1 - co), cond)

    for c in range(NC):
        place(Q, c)
        for h in range(HC):
            cols = slice(h * HS, (h + 1) * HS)
            q, k, v = (b["f"][a, c, :, cols] for a in (Q, K, V))
            p = (mm(q, k, 1, 1) * b["doc"][...]).astype(BF16)
            b["pm"][c, :, cols] = p
            wide = jnp.concatenate([p, q * b["mk"][CAR]], axis=1)
            attn = mm(wide, jnp.concatenate([v, b["st"][c, :, cols]], axis=0), 1, 0)
            gain_h = gain[:, (c * HC + h) * HS : (c * HC + h + 1) * HS]
            scale = lax.rsqrt(jnp.mean(attn * attn, axis=-1, keepdims=True) + NORM_EPS)
            unit = attn * scale
            b["nb"][c, d, co, :, cols] = (unit * gain_h).astype(BF16)
            g = b["dn"][c, :, cols] * gain_h
            d_attn = scale * (g - unit * jnp.mean(g * unit, axis=-1, keepdims=True))
            d_half = d_attn.astype(BF16)
            b["dh"][c, :, cols] = d_half
        spread(c, d, d < D - 1, d > 0)
        share(c, d, None)
        write(0, c, b["nb"].at[c, d, co], normed_out)
        for h in range(HC):
            cols = slice(h * HS, (h + 1) * HS)
            b["rf"][c, :, cols] = mm(b["f"][Q, c, :, cols] * b["mk"][HEAD], b["dh"][c, :, cols], 0, 0)
        copy = remote(
            b["lr"].at[c], b["rst"].at[c], b["v_ss"].at[c], b["v_rs"].at[c], seq=lax.rem(s + S - 1, S)
        )
        v_copies.append(copy)

        @pl.when(s == S - 1)
        def _(copy=copy, c=c):
            b["lr"][c] = b["rf"][c].astype(BF16)
            copy.start()

    def pass_on(c):
        copy = v_copies[c]

        @pl.when(s < S - 1)
        def _():
            copy.wait_recv()
            join = jnp.broadcast_to(b["jn"][1][0:1, 0:1], (HS, CW))
            b["lr"][c] = (b["rf"][c] + jnp.where(join > 0.5, b["rst"][c].astype(F32), 0.0)).astype(BF16)

        pl.when((s < S - 1) & (s > 0))(copy.start)
        sent.append((s > 0, copy))

    def arrived(c, origin):
        block = b["nb"].at[c, origin, co]
        remote(block, block, b["nr_ss"].at[c, origin], b["n_rs"].at[c, origin], dp=lax.rem(d + 1, D)).wait_recv()

    def relay(c, step):
        @pl.when(d - step >= 0)
        def _():
            arrived(c, d - step)

        spread(c, jnp.maximum(d - step, 0), (d - step >= 0) & (d < D - 1), None)
        share(c, jnp.maximum(d - step, 0), d - step >= 0)

        @pl.when(d + step < D)
        def _():
            arrived(c, d + step)

        spread(c, jnp.minimum(d + step, D - 1), None, (d + step < D) & (d > 0))
        share(c, jnp.minimum(d + step, D - 1), d + step < D)

    def backward(c):
        for h in range(HC):
            cols = slice(h * HS, (h + 1) * HS)
            q, k, v = (b["f"][a, c, :, cols] for a in (Q, K, V))
            dh, p = b["dh"][c, :, cols], b["pm"][c, :, cols]
            st, rst = b["st"][c, :, cols], b["rst"][c, :, cols]
            dp = (mm(dh, v, 1, 1) * b["doc"][...]).astype(BF16)
            rev = b["mk"][REV]
            b["do"][0, c, :, cols] = (mm(dp, k, 1, 0) + mm(dh * b["mk"][CAR], st, 1, 1)).astype(BF16)
            b["do"][1, c, :, cols] = (mm(dp, q, 0, 0) + mm(v * rev, rst, 1, 1)).astype(BF16)
            b["do"][2, c, :, cols] = (mm(p, dh, 0, 0) + mm(k * rev, rst, 1, 0)).astype(BF16)
        for i, out in enumerate((dq_out, dk_out, dv_out)):
            write(1 + i, c, b["do"].at[i, c], out)

    x_copies = {}

    def weigh(c):
        mate = 1 - co
        for o in range(D):
            block = b["nb"].at[c, o, mate]
            remote(block, block, b["p_ss"].at[c, o], b["p_rs"].at[c, o], seq=xi * 2 + 1 - co).wait_recv()
        right = b["nb"][c].reshape(D * 2 * R, CW)
        for t in list(range(1, X)) + [0]:
            to = lax.rem(xi + t, X)
            part = mm(b["lhs"][to], right, 1, 0)
            if t == 0:
                b["acc"][c] = part
                continue
            b["xs"][c, t - 1] = part.astype(BF16)
            copy = remote(
                b["xs"].at[c, t - 1],
                b["xr"].at[c, t - 1],
                b["x_ss"].at[c, t - 1],
                b["x_rs"].at[c, t - 1],
                seq=to * 2 + co,
            )
            go(copy)
            x_copies[c, t] = copy

    def settle(c):
        for t in range(1, X):
            x_copies[c, t].wait_recv()
            b["acc"][c] = b["acc"][c] + b["xr"][c, t - 1].astype(F32)
        write(4, c, b["acc"].at[c], wg_out)

    for c in range(NC):
        pass_on(c)
        if D > 1:
            relay(c, 1)
    for copy in b_copies:
        copy.wait_recv()
    for o in range(D):
        for cc in range(2):
            at = (o * 2 + cc) * R
            b["lhs"][:, :, at : at + R] = b["gz"][o, cc]
    for c in range(NC):
        backward(c)
        if D > 2:
            relay(c, 2)
    for step in range(3, D - 1):
        for c in range(NC):
            relay(c, step)
    for c in range(NC):
        if D > 3:
            relay(c, D - 1)
        weigh(c)
        if c:
            settle(c - 1)
    settle(NC - 1)
    for copy in outs:
        copy.wait()
    for cond, copy in sent:
        when(cond, copy.wait_send)


def solution(mesh):
    def local(queries, key_rows, value_rows, row_plan, segments, norm_gain, out_weight, out_grad):
        rows, width = queries.shape
        z = plan_sizes(mesh, rows, width, out_grad.shape[1])
        scratch = scratch_of(z)
        half = jax.ShapeDtypeStruct((rows, width), BF16)
        anywhere = pl.BlockSpec(memory_space=pl.ANY)
        vmem = pl.BlockSpec(memory_space=pltpu.VMEM)
        smem = pl.BlockSpec(memory_space=pltpu.SMEM)
        return pl.pallas_call(
            functools.partial(whole_body, z, tuple(scratch)),
            out_shape=[half, half, half, half, jax.ShapeDtypeStruct((z["RB"], width), F32)],
            in_specs=[smem, vmem, vmem] + [anywhere] * 5,
            out_specs=[anywhere] * 5,
            scratch_shapes=list(scratch.values()),
            compiler_params=pltpu.CompilerParams(
                collective_id=0, has_side_effects=True, vmem_limit_bytes=60 * 1024 * 1024
            ),
        )(row_plan, segments, norm_gain.reshape(1, width), queries, key_rows, value_rows, out_weight, out_grad)

    placed = (
        P(("dp", "seq"), "mp"),
        P(("dp", "seq"), "mp"),
        P(("dp", "seq"), "mp"),
        P(),
        P("dp", "seq"),
        P("mp"),
        P("mp", None),
        P(("dp", "seq"), "mp"),
    )
    return jax.shard_map(
        local, mesh=mesh, in_specs=placed, out_specs=(P(("dp", "seq"), "mp"),) * 5, check_vma=False
    )
```

```python
import functools

import jax
import jax.numpy as jnp
from jax import lax
from jax.experimental import pallas as pl
from jax.experimental.pallas import tpu as pltpu
from jax.sharding import PartitionSpec as P

HS = 128
NORM_EPS = 1e-06
F32 = jnp.float32
BF16 = jnp.bfloat16
MESH = pl.DeviceIdType.MESH
K, V, Q = 0, 1, 2


def mm(a, b, ca, cb):
    return lax.dot_general(a, b, (((ca,), (cb,)), ((), ())), preferred_element_type=F32)


def plan_sizes(mesh, rows, width, out_half):
    groups, shards, splits = mesh.shape["dp"], mesh.shape["seq"], mesh.shape["mp"]
    z = {}
    z["D"], z["S"], z["M"], z["X"] = groups, shards, splits, shards // 2
    z["R"], z["W"], z["DM"] = rows, width, out_half
    z["DOUT"] = out_half * splits
    heads = width // HS
    z["HC"] = 4 if heads % 4 == 0 else 1
    z["NC"] = heads // z["HC"]
    z["CW"] = z["HC"] * HS
    z["CAP"] = rows // min(groups, 8) + rows // 16
    z["CP"] = -(-z["CAP"] // 16) * 16
    z["RB"] = z["DOUT"] // (groups * shards)
    z["PX"] = splits // z["X"]
    z["RP"] = z["RB"] // z["PX"]
    return z


def scratch_of(z):
    D, M, X, R, W, NC, CW = (z[n] for n in ("D", "M", "X", "R", "W", "NC", "CW"))
    XO = max(1, X - 1)
    vm = pltpu.VMEM
    dma = pltpu.SemaphoreType.DMA
    return dict(
        x=vm((3, R, W), BF16),
        snd=vm((3, NC, D, z["CP"], CW), BF16),
        arr=vm((3, NC, D, z["CP"], CW), BF16),
        f=vm((3, NC, R, CW), BF16),
        w=vm((NC, CW, z["DOUT"]), BF16),
        g=vm((M, R, z["DM"]), BF16),
        gt=vm((z["DOUT"], R), BF16),
        gz=vm((D, 2, X, z["RB"], R), BF16),
        plan=pltpu.SMEM((D, D), jnp.int32),
        segi=vm((1, R), jnp.int32),
        gain=vm((1, W), F32),
        dn=vm((NC, R, CW), F32),
        pm=vm((NC, R, CW), BF16),
        lf=vm((HS, CW), F32),
        ls=vm((NC, HS, CW), BF16),
        st=vm((NC, HS, CW), BF16),
        rf=vm((NC, HS, CW), F32),
        lr=vm((NC, HS, CW), BF16),
        rst=vm((NC, HS, CW), BF16),
        dh=vm((NC, R, CW), BF16),
        nb=vm((NC, D, 2, R, CW), BF16),
        acc=vm((NC, X, z["RB"], CW), F32),
        xs=vm((NC, XO, z["RB"], CW), BF16),
        xr=vm((NC, XO, z["RB"], CW), BF16),
        seg=vm((3, 8, R), F32),
        doc=vm((R, R), F32),
        mk=vm((4, R, R), BF16),
        jn=vm((2, 8, R), F32),
        sel=vm((D * z["CP"], R), BF16),
        pick=vm((R, D * z["CP"]), BF16),
        in_s=dma((7,)),
        w_s=dma((NC,)),
        y_ss=dma((max(1, M - 1),)),
        y_rs=dma((max(1, M - 1),)),
        sg_ss=dma((2,)),
        sg_rs=dma((2,)),
        r_ss=dma((3, NC, D)),
        r_rs=dma((3, NC, D)),
        g_ss=dma((2 * D,)),
        g_rs=dma((2 * D,)),
        b_ss=dma((max(1, M - 1),)),
        b_rs=dma((max(1, M - 1),)),
        f_ss=dma((NC,)),
        f_rs=dma((NC,)),
        v_ss=dma((NC,)),
        v_rs=dma((NC,)),
        nr_ss=dma((NC, D)),
        nl_ss=dma((NC, D)),
        n_rs=dma((NC, D)),
        p_ss=dma((NC, D)),
        p_rs=dma((NC, D)),
        x_ss=dma((NC, XO, 2)),
        x_rs=dma((NC, XO, 2)),
    )


TAIL, HEAD, CAR, REV = 0, 1, 2, 3


def whole_body(z, names, *refs):
    plan_in, seg_in, gain_in, q_in, k_in, v_in, w_in, g_in = refs[:8]
    normed_out, grads_out, wg_out = refs[8:11]
    b = dict(zip(names, refs[11:]))
    plan, gain = b["plan"], b["gain"]
    D, S, M, X, R, NC, CW, HC = (z[n] for n in ("D", "S", "M", "X", "R", "NC", "CW", "HC"))
    CAP, CP, RB, RP, PX, DM = (z[n] for n in ("CAP", "CP", "RB", "RP", "PX", "DM"))
    d, s, m = lax.axis_index("dp"), lax.axis_index("seq"), lax.axis_index("mp")
    xi, co = s // 2, s % 2
    sent = []

    def remote(src, dst, ss, rs, **where):
        return pltpu.make_async_remote_copy(
            src_ref=src, dst_ref=dst, send_sem=ss, recv_sem=rs, device_id=where, device_id_type=MESH
        )

    def when(cond, act):
        if cond is None:
            act()
        else:
            pl.when(cond)(act)

    def go(copy, cond=None):
        when(cond, copy.start)
        sent.append((cond, copy))

    barrier = pltpu.get_barrier_semaphore()
    peers = 0

    def greet(**where):
        pl.semaphore_signal(barrier, inc=1, device_id=where, device_id_type=MESH)

    sources = (
        (plan_in, plan),
        (k_in, b["x"].at[K]),
        (v_in, b["x"].at[V]),
        (g_in, b["g"].at[m]),
        (seg_in, b["segi"]),
        (q_in, b["x"].at[Q]),
        (gain_in, gain),
    )
    loads = [pltpu.make_async_copy(a, c, b["in_s"].at[i]) for i, (a, c) in enumerate(sources)]
    for load in loads:
        load.start()
    w_loads = [
        pltpu.make_async_copy(w_in.at[pl.ds(c * CW, CW), :], b["w"].at[c], b["w_s"].at[c])
        for c in range(NC)
    ]

    if CP > CAP:
        b["arr"][:, :, :, CAP:CP, :] = jnp.zeros((3, NC, D, CP - CAP, CW), BF16)

    @pl.when(s == 0)
    def _():
        b["seg"][1] = jnp.full((8, R), -1.0, F32)
        b["st"][...] = jnp.zeros_like(b["st"])

    @pl.when(s == S - 1)
    def _():
        b["seg"][2] = jnp.full((8, R), -1.0, F32)
        b["rst"][...] = jnp.zeros_like(b["rst"])

    for t in range(D):
        for cc in range(2):
            if t or cc:
                greet(dp=lax.rem(d + t, D), seq=xi * 2 + (co + cc) % 2, mp=m)
                peers += 1
    for t in range(1, X):
        for cc in range(2):
            greet(dp=d, seq=lax.rem(xi + t, X) * 2 + cc, mp=m)
            peers += 1
    for t in range(1, M):
        greet(dp=d, seq=s, mp=lax.rem(m + t, M))
        peers += 1

    loads[0].wait()
    slot = lax.broadcasted_iota(jnp.int32, (D * CP, R), 0)
    row = lax.broadcasted_iota(jnp.int32, (D * CP, R), 1)
    start = jnp.int32(0)
    hot = jnp.zeros((D * CP, R), F32)
    for j in range(D):
        inside = (slot >= j * CP) & (slot < j * CP + CAP) & (row - start == slot - j * CP)
        hot = jnp.where(inside, 1.0, hot)
        start = start + plan[d, j]
    b["sel"][...] = hot.astype(BF16)
    slot = lax.broadcasted_iota(jnp.int32, (R, D * CP), 1)
    row = lax.broadcasted_iota(jnp.int32, (R, D * CP), 0)
    start = jnp.int32(0)
    hot = jnp.zeros((R, D * CP), F32)
    for i in range(D):
        count = plan[i, d]
        at = slot - i * CP
        inside = (at >= 0) & (at < CP) & (at == row - start) & (row - start < count)
        hot = jnp.where(inside, 1.0, hot)
        start = start + count
    b["pick"][...] = hot.astype(BF16)

    pl.semaphore_wait(barrier, peers)

    loads[3].wait()
    y_copies = []
    for t in range(1, M):
        c = remote(
            b["g"].at[m], b["g"].at[m], b["y_ss"].at[t - 1], b["y_rs"].at[t - 1], mp=lax.rem(m + t, M)
        )
        go(c)
        y_copies.append(c)
    loads[4].wait()
    b["seg"][0] = jnp.broadcast_to(b["segi"][...].astype(F32), (8, R))
    after = remote(b["seg"].at[0], b["seg"].at[1], b["sg_ss"].at[0], b["sg_rs"].at[0], seq=lax.rem(s + 1, S))
    before = remote(
        b["seg"].at[0], b["seg"].at[2], b["sg_ss"].at[1], b["sg_rs"].at[1], seq=lax.rem(s + S - 1, S)
    )
    go(after, s < S - 1)
    go(before, s > 0)

    r_copies = {}

    def hand(a, c):
        packed = mm(b["sel"][...], b["x"][a, :, c * CW : (c + 1) * CW], 1, 0).astype(BF16)
        b["snd"][a, c] = packed.reshape(D, CP, CW)
        for t in range(1, D):
            to = lax.rem(d + t, D)
            copy = remote(
                b["snd"].at[a, c, to, pl.ds(0, CAP)],
                b["arr"].at[a, c, d, pl.ds(0, CAP)],
                b["r_ss"].at[a, c, t],
                b["r_rs"].at[a, c, t],
                dp=to,
            )
            go(copy)
            r_copies[a, c, t] = copy
        b["arr"][a, c, d] = b["snd"][a, c, d]

    loads[1].wait()
    loads[2].wait()
    for c in range(NC):
        hand(K, c)
        hand(V, c)
    for c in range(NC):
        w_loads[c].start()
    loads[5].wait()
    for c in range(NC):
        hand(Q, c)

    pl.when(s > 0)(after.wait_recv)
    pl.when(s < S - 1)(before.wait_recv)
    across = jnp.broadcast_to(b["seg"][0][0:1, :], (R, R))
    down = jnp.transpose(across)
    t_at = lax.broadcasted_iota(jnp.int32, (R, R), 0)
    u_at = lax.broadcasted_iota(jnp.int32, (R, R), 1)
    b["doc"][...] = jnp.where((u_at <= t_at) & (across == down), 1.0, 0.0)
    own_last = b["seg"][0][0:1, R - 1 : R]
    own_first = b["seg"][0][0:1, 0:1]
    last_before = b["seg"][1][0:1, R - 1 : R]
    first_after = b["seg"][2][0:1, 0:1]
    for i, value in ((TAIL, own_last), (HEAD, own_first), (CAR, last_before), (REV, first_after)):
        b["mk"][i] = jnp.where(down == jnp.broadcast_to(value, (R, R)), 1.0, 0.0).astype(BF16)
    for i, (one, two) in enumerate(((own_last, last_before), (own_first, first_after))):
        b["jn"][i] = jnp.broadcast_to(jnp.where(one == two, 1.0, 0.0), (8, R))

    for c in y_copies:
        c.wait_recv()
    for i in range(M):
        for j in range(DM // HS):
            b["gt"][pl.ds(i * DM + j * HS, HS), :] = jnp.transpose(b["g"][i, :, j * HS : (j + 1) * HS])
    px, off = m // PX, pl.multiple_of((m % PX) * RP, RP)
    g_copies = []
    for t in range(D):
        for cc in range(2):
            to, core = lax.rem(d + t, D), (co + cc) % 2
            at = pl.multiple_of(((to * X + px) * 2 + core) * RB + off, RP)
            if t == 0 and cc == 0:
                b["gz"][d, co, px, pl.ds(off, RP), :] = b["gt"][pl.ds(at, RP), :]
                continue
            copy = remote(
                b["gt"].at[pl.ds(at, RP), :],
                b["gz"].at[d, co, px, pl.ds(off, RP), :],
                b["g_ss"].at[t * 2 + cc],
                b["g_rs"].at[t * 2 + cc],
                dp=to,
                seq=xi * 2 + core,
            )
            go(copy)
            g_copies.append(copy)

    for c in range(NC):
        w_loads[c].wait()

    def grow(c, carry):
        total = mm(b["g"][0], b["w"][c, :, 0:DM], 1, 1)
        for i in range(1, M):
            total = total + mm(b["g"][i], b["w"][c, :, i * DM : (i + 1) * DM], 1, 1)
        b["dn"][c] = total
        return carry

    lax.fori_loop(0, NC, grow, 0)

    def place(a, c):
        for t in range(1, D):
            r_copies[a, c, t].wait_recv()
        parts = b["arr"][a, c].reshape(D * CP, CW)
        b["f"][a, c] = mm(b["pick"][...], parts, 1, 0).astype(BF16)

    for c in range(NC):
        place(K, c)
        place(V, c)
        for h in range(HC):
            cols = slice(h * HS, (h + 1) * HS)
            b["lf"][:, cols] = mm(b["f"][K, c, :, cols] * b["mk"][TAIL], b["f"][V, c, :, cols], 0, 0)
        copy = remote(
            b["ls"].at[c], b["st"].at[c], b["f_ss"].at[c], b["f_rs"].at[c], seq=lax.rem(s + 1, S)
        )
        pl.when(s > 0)(copy.wait_recv)
        join = jnp.broadcast_to(b["jn"][0][0:1, 0:1], (HS, CW))
        b["ls"][c] = (b["lf"][...] + jnp.where(join > 0.5, b["st"][c].astype(F32), 0.0)).astype(BF16)
        go(copy, s < S - 1)

    v_copies = []
    loads[6].wait()

    def spread(c, origin, right, left):
        block = b["nb"].at[c, origin, co]
        if right is not None:
            go(remote(block, block, b["nr_ss"].at[c, origin], b["n_rs"].at[c, origin], dp=jnp.minimum(d + 1, D - 1)), right)
        if left is not None:
            go(remote(block, block, b["nl_ss"].at[c, origin], b["n_rs"].at[c, origin], dp=jnp.maximum(d - 1, 0)), left)

    def share(c, origin, cond):
        block = b["nb"].at[c, origin, co]
        go(remote(block, block, b["p_ss"].at[c, origin], b["p_rs"].at[c, origin], seq=xi * 2 + 1 - co), cond)

    for c in range(NC):
        place(Q, c)
        for h in range(HC):
            cols = slice(h * HS, (h + 1) * HS)
            q, k, v = (b["f"][a, c, :, cols] for a in (Q, K, V))
            p = (mm(q, k, 1, 1) * b["doc"][...]).astype(BF16)
            b["pm"][c, :, cols] = p
            wide = jnp.concatenate([p, q * b["mk"][CAR]], axis=1)
            attn = mm(wide, jnp.concatenate([v, b["st"][c, :, cols]], axis=0), 1, 0)
            gain_h = gain[:, (c * HC + h) * HS : (c * HC + h + 1) * HS]
            scale = lax.rsqrt(jnp.mean(attn * attn, axis=-1, keepdims=True) + NORM_EPS)
            unit = attn * scale
            out = (unit * gain_h).astype(BF16)
            b["nb"][c, d, co, :, cols] = out
            normed_out[c, :, cols] = out
            g = b["dn"][c, :, cols] * gain_h
            d_attn = scale * (g - unit * jnp.mean(g * unit, axis=-1, keepdims=True))
            d_half = d_attn.astype(BF16)
            b["dh"][c, :, cols] = d_half
        spread(c, d, d < D - 1, d > 0)
        share(c, d, None)
        for h in range(HC):
            cols = slice(h * HS, (h + 1) * HS)
            b["rf"][c, :, cols] = mm(b["f"][Q, c, :, cols] * b["mk"][HEAD], b["dh"][c, :, cols], 0, 0)
        copy = remote(
            b["lr"].at[c], b["rst"].at[c], b["v_ss"].at[c], b["v_rs"].at[c], seq=lax.rem(s + S - 1, S)
        )
        v_copies.append(copy)

        @pl.when(s == S - 1)
        def _(copy=copy, c=c):
            b["lr"][c] = b["rf"][c].astype(BF16)
            copy.start()

    def pass_on(c):
        copy = v_copies[c]

        @pl.when(s < S - 1)
        def _():
            copy.wait_recv()
            join = jnp.broadcast_to(b["jn"][1][0:1, 0:1], (HS, CW))
            b["lr"][c] = (b["rf"][c] + jnp.where(join > 0.5, b["rst"][c].astype(F32), 0.0)).astype(BF16)

        pl.when((s < S - 1) & (s > 0))(copy.start)
        sent.append((s > 0, copy))

    def arrived(c, origin):
        block = b["nb"].at[c, origin, co]
        remote(block, block, b["nr_ss"].at[c, origin], b["n_rs"].at[c, origin], dp=lax.rem(d + 1, D)).wait_recv()

    def relay(c, step):
        @pl.when(d - step >= 0)
        def _():
            arrived(c, d - step)

        spread(c, jnp.maximum(d - step, 0), (d - step >= 0) & (d < D - 1), None)
        share(c, jnp.maximum(d - step, 0), d - step >= 0)

        @pl.when(d + step < D)
        def _():
            arrived(c, d + step)

        spread(c, jnp.minimum(d + step, D - 1), None, (d + step < D) & (d > 0))
        share(c, jnp.minimum(d + step, D - 1), d + step < D)

    def backward(c):
        for h in range(HC):
            cols = slice(h * HS, (h + 1) * HS)
            q, k, v = (b["f"][a, c, :, cols] for a in (Q, K, V))
            dh, p = b["dh"][c, :, cols], b["pm"][c, :, cols]
            st, rst = b["st"][c, :, cols], b["rst"][c, :, cols]
            dp = (mm(dh, v, 1, 1) * b["doc"][...]).astype(BF16)
            rev = b["mk"][REV]
            grads_out[0, c, :, cols] = (mm(dp, k, 1, 0) + mm(dh * b["mk"][CAR], st, 1, 1)).astype(BF16)
            grads_out[1, c, :, cols] = (mm(dp, q, 0, 0) + mm(v * rev, rst, 1, 1)).astype(BF16)
            grads_out[2, c, :, cols] = (mm(p, dh, 0, 0) + mm(k * rev, rst, 1, 0)).astype(BF16)

    def add(c, origin, t, cols, fresh=False):
        to = lax.rem(xi + t, X)
        left = jnp.concatenate([b["gz"][origin, 0, to], b["gz"][origin, 1, to]], axis=1)
        right = b["nb"][c, origin, :, :, cols].reshape(2 * R, cols.stop - cols.start)
        term = mm(left, right, 1, 0)
        b["acc"][c, t, :, cols] = term if fresh else b["acc"][c, t, :, cols] + term

    everything = slice(0, CW)
    pieces = (slice(0, CW // 2), slice(CW // 2, CW)) if CW % (2 * HS) == 0 else (everything,)

    def paired(c, origin):
        block = b["nb"].at[c, origin, 1 - co]
        remote(block, block, b["p_ss"].at[c, origin], b["p_rs"].at[c, origin], seq=xi * 2 + 1 - co).wait_recv()

    def each(step, act):
        if step == 0:
            act(d)
            return
        pl.when(d - step >= 0)(lambda: act(d - step))
        pl.when(d + step < D)(lambda: act(d + step))

    def absorb(c, step):
        def one(origin):
            paired(c, origin)
            for t in range(X):
                add(c, origin, t, everything, fresh=step == 0)

        each(step, one)

    x_copies = {}

    def close(c, step):
        each(step, lambda origin: paired(c, origin))
        for t in list(range(1, X)) + [0]:
            for i, cols in enumerate(pieces):
                each(step, lambda origin: add(c, origin, t, cols, fresh=step == 0))
                if t == 0:
                    continue
                b["xs"][c, t - 1, :, cols] = b["acc"][c, t, :, cols].astype(BF16)
                part = pl.ds(cols.start, cols.stop - cols.start)
                copy = remote(
                    b["xs"].at[c, t - 1, :, part],
                    b["xr"].at[c, t - 1, :, part],
                    b["x_ss"].at[c, t - 1, i],
                    b["x_rs"].at[c, t - 1, i],
                    seq=lax.rem(xi + t, X) * 2 + co,
                )
                go(copy)
                x_copies[c, t, i] = copy

    def settle(c):
        for i, cols in enumerate(pieces):
            total = b["acc"][c, 0, :, cols]
            for t in range(1, X):
                x_copies[c, t, i].wait_recv()
                total = total + b["xr"][c, t - 1, :, cols].astype(F32)
            wg_out[c, :, cols] = total

    for copy in g_copies:
        copy.wait_recv()
    b_copies = []
    part = b["gz"].at[:, :, px, pl.ds(off, RP), :]
    for t in range(1, M):
        copy = remote(part, part, b["b_ss"].at[t - 1], b["b_rs"].at[t - 1], mp=lax.rem(m + t, M))
        go(copy)
        b_copies.append(copy)

    for c in range(NC):
        pass_on(c)
    for c in range(NC):
        if D > 1:
            relay(c, 1)
        backward(c)
    for copy in b_copies:
        copy.wait_recv()
    last = D - 1
    for step in range(2, last):
        for c in range(NC):
            relay(c, step)
            if step == 2:
                absorb(c, 0)
            absorb(c, step - 1)
    for c in range(NC):
        if last > 1:
            relay(c, last)
        if last in (1, 2):
            absorb(c, 0)
        if last > 1:
            absorb(c, last - 1)
        close(c, last)
        if c:
            settle(c - 1)
    settle(NC - 1)
    for cond, copy in sent:
        when(cond, copy.wait_send)


def write_body(n_chunks, normed, grads, wg, *refs):
    outs, sem = refs[:5], refs[5]
    width = normed.shape[2]
    copies = []
    for c in range(n_chunks):
        cols = pl.ds(c * width, width)
        parts = (normed.at[c], grads.at[0, c], grads.at[1, c], grads.at[2, c], wg.at[c])
        for i, (part, out) in enumerate(zip(parts, outs)):
            copies.append(pltpu.make_async_copy(part, out.at[:, cols], sem.at[c, i]))
    for copy in copies:
        copy.start()
    for copy in copies:
        copy.wait()


def solution(mesh):
    def local(queries, key_rows, value_rows, row_plan, segments, norm_gain, out_weight, out_grad):
        rows, width = queries.shape
        z = plan_sizes(mesh, rows, width, out_grad.shape[1])
        scratch = scratch_of(z)
        chunks, span = z["NC"], z["CW"]
        anywhere = pl.BlockSpec(memory_space=pl.ANY)
        vmem = pl.BlockSpec(memory_space=pltpu.VMEM)
        operands = (
            row_plan,
            segments,
            norm_gain.reshape(1, width),
            queries,
            key_rows,
            value_rows,
            out_weight,
            out_grad,
        )
        kept = pl.pallas_call(
            functools.partial(whole_body, z, tuple(scratch)),
            out_shape=[
                pltpu.VMEM((chunks, rows, span), BF16),
                pltpu.VMEM((3, chunks, rows, span), BF16),
                pltpu.VMEM((chunks, z["RB"], span), F32),
            ],
            in_specs=[pl.BlockSpec(memory_space=pltpu.HBM)] * 8,
            out_specs=[vmem] * 3,
            scratch_shapes=list(scratch.values()),
            compiler_params=pltpu.CompilerParams(
                collective_id=0, has_side_effects=True, vmem_limit_bytes=50 * 1024 * 1024
            ),
        )(*(pltpu.with_memory_space_constraint(a, pltpu.HBM) for a in operands))
        half = jax.ShapeDtypeStruct((rows, width), BF16)
        return pl.pallas_call(
            functools.partial(write_body, chunks),
            out_shape=[half, half, half, half, jax.ShapeDtypeStruct((z["RB"], width), F32)],
            in_specs=[anywhere] * 3,
            out_specs=[anywhere] * 5,
            scratch_shapes=[pltpu.SemaphoreType.DMA((chunks, 5))],
            compiler_params=pltpu.CompilerParams(vmem_limit_bytes=4 * 1024 * 1024),
        )(*kept)

    placed = (
        P(("dp", "seq"), "mp"),
        P(("dp", "seq"), "mp"),
        P(("dp", "seq"), "mp"),
        P(),
        P("dp", "seq"),
        P("mp"),
        P("mp", None),
        P(("dp", "seq"), "mp"),
    )
    return jax.shard_map(
        local, mesh=mesh, in_specs=placed, out_specs=(P(("dp", "seq"), "mp"),) * 5, check_vma=False
    )
```

```python
import functools

import jax
import jax.numpy as jnp
from jax import lax
from jax.experimental import pallas as pl
from jax.experimental.pallas import tpu as pltpu
from jax.sharding import PartitionSpec as P

HS = 128
NORM_EPS = 1e-06
F32 = jnp.float32
BF16 = jnp.bfloat16
MESH = pl.DeviceIdType.MESH
K, V, Q = 0, 1, 2
SPAN = 4
TERMS = 1
STEP = 2


def mm(a, b, ca, cb):
    return lax.dot_general(a, b, (((ca,), (cb,)), ((), ())), preferred_element_type=F32)


def plan_sizes(mesh, rows, width, out_half):
    groups, shards, splits = mesh.shape["dp"], mesh.shape["seq"], mesh.shape["mp"]
    z = {}
    z["D"], z["S"], z["M"], z["X"] = groups, shards, splits, shards // 2
    z["R"], z["W"], z["DM"] = rows, width, out_half
    z["DOUT"] = out_half * splits
    heads = width // HS
    full, rest = divmod(heads, SPAN)
    z["HEADS"] = [SPAN] * full + [rest] * (rest > 0)
    z["NC"] = len(z["HEADS"])
    z["CW"] = max(z["HEADS"]) * HS
    z["CAP"] = rows // min(groups, 8) + rows // 16
    z["CP"] = -(-z["CAP"] // 16) * 16
    z["RB"] = z["DOUT"] // (groups * shards)
    z["PX"] = splits // z["X"]
    z["RP"] = z["RB"] // z["PX"]
    return z


def scratch_of(z):
    D, M, X, R, W, NC, CW = (z[n] for n in ("D", "M", "X", "R", "W", "NC", "CW"))
    XO, SO = max(1, X - 1), max(1, z["S"] - 1)
    vm = pltpu.VMEM
    dma = pltpu.SemaphoreType.DMA
    return dict(
        x=vm((3, R, W), BF16),
        snd=vm((3, NC, D, z["CP"], CW), BF16),
        arr=vm((3, NC, D, z["CP"], CW), BF16),
        f=vm((3, NC, R, CW), BF16),
        w=vm((NC, CW, z["DOUT"]), BF16),
        g=vm((M, R, z["DM"]), BF16),
        gt=vm((z["DOUT"], R), BF16),
        gz=vm((D, 2, X, z["RB"], R), BF16),
        plan=pltpu.SMEM((D, D), jnp.int32),
        segi=vm((1, R), jnp.int32),
        gain=vm((1, W), F32),
        dn=vm((NC, R, CW), F32),
        pm=vm((NC, R, CW), BF16),
        tot=vm((HS, CW), F32),
        ls=vm((NC, HS, CW), BF16),
        sr=vm((NC, SO, HS, CW), BF16),
        st=vm((NC, HS, CW), BF16),
        lr=vm((NC, HS, CW), BF16),
        rr=vm((NC, SO, HS, CW), BF16),
        rst=vm((NC, HS, CW), BF16),
        dh=vm((NC, R, CW), BF16),
        nb=vm((NC, D, 2, R, CW), BF16),
        acc=vm((NC, X, z["RB"], CW), F32),
        xs=vm((NC, XO, z["RB"], CW), BF16),
        xr=vm((NC, XO, z["RB"], CW), BF16),
        seg=vm((2 * SO + 1, 8, R), F32),
        doc=vm((R, R), F32),
        mk=vm((4, R, R), BF16),
        jn=vm((2 * SO, 8, R), F32),
        sel=vm((D * z["CP"], R), BF16),
        pick=vm((R, D * z["CP"]), BF16),
        in_s=dma((7,)),
        w_s=dma((NC,)),
        y_ss=dma((max(1, M - 1),)),
        y_rs=dma((max(1, M - 1),)),
        sg_ss=dma((2 * SO,)),
        sg_rs=dma((2 * SO,)),
        r_ss=dma((3, NC, D)),
        r_rs=dma((3, NC, D)),
        g_ss=dma((2 * D,)),
        g_rs=dma((2 * D,)),
        b_ss=dma((max(1, M - 1),)),
        b_rs=dma((max(1, M - 1),)),
        f_ss=dma((NC, SO)),
        f_rs=dma((NC, SO)),
        v_ss=dma((NC, SO)),
        v_rs=dma((NC, SO)),
        nr_ss=dma((NC, D)),
        nl_ss=dma((NC, D)),
        n_rs=dma((NC, D)),
        p_ss=dma((NC, D)),
        p_rs=dma((NC, D)),
        x_ss=dma((NC, XO, 2)),
        x_rs=dma((NC, XO, 2)),
    )


TAIL, HEAD, CAR, REV = 0, 1, 2, 3


def order(n, groups):
    last = groups - 1
    steps = []

    def do(name, *args):
        steps.append((name, *args))

    def rows(act, c, *names):
        for a in names if c < n else ():
            do(act, a, c)

    rows("pack", 0, K)
    rows("send", 0, K)
    rows("pack", 0, V)
    rows("send", 0, V)
    do("fetch")
    for c in range(2):
        rows("pack", c + 1, K, V)
        rows("send", c + 1, K, V)
        rows("pack", c, Q)
        rows("send", c, Q)
    do("masks")
    for c in range(2, n):
        rows("pack", c + 1, K, V)
        rows("pack", c, Q)
    do("turn")
    for c in range(min(2, n)):
        do("grow", c)
        do("keep", c)
    early = []
    left = [(STEP * k + c, c, k) for c in range(n) for k in range(1, last + 1)]
    for c in range(n):
        do("forward", c)
        if c == TERMS:
            do("terms")
        rows("send", c + 3, K, V)
        rows("send", c + 2, Q)
        if c + 2 < n:
            do("grow", c + 2)
        if 1 <= c < n - 1 and last:
            do("relay", c - 1, 1)
            left.remove((STEP + c - 1, c - 1, 1))
            early.append((c - 1, 0))
        if c + 2 < n:
            do("keep", c + 2)
        if 2 <= c < n - 1:
            do("backward", c - 2)
    if n <= TERMS:
        do("terms")
    do("double")
    behind, closed, due, ready = list(range(max(0, n - 3), n)), [], early, False

    def finish(c):
        if ("doubled",) not in steps:
            do("doubled")
        for item in [item for item in due if item[0] == c]:
            do("absorb", *item)
            due.remove(item)
        do("close", c)
        closed.append(c)
        if len(closed) > 1:
            do("settle", closed[-2])

    for _, c, k in sorted(left):
        if (c, k) == (n - 1, last):
            while behind:
                do("backward", behind.pop(0))
        do("relay", c, k)
        if (c, k) == (n - 2, 1):
            do("backward", behind.pop(0))
        if (c, k) == (n - 1, 1):
            if ("doubled",) not in steps:
                do("doubled")
            ready = True
        if k == 1:
            due.append((c, 0))
        else:
            due.append((c, k - 1))
        if ready:
            for item in [item for item in due if item[0] == due[0][0] and item[1] < last - 1][:2]:
                do("absorb", *item)
                due.remove(item)
        if (c, k) == (n - 1, last - 1) and behind:
            do("backward", behind.pop(0))
        if k == last:
            finish(c)
    if not last:
        due.extend((c, 0) for c in range(n))
        for c in range(n):
            finish(c)
    while behind:
        do("backward", behind.pop(0))
    if closed:
        do("settle", closed[-1])
    return steps


def whole_body(z, names, *refs):
    plan_in, seg_in, gain_in, q_in, k_in, v_in, w_in, g_in = refs[:8]
    normed_out, grads_out, wg_out = refs[8:11]
    b = dict(zip(names, refs[11:]))
    plan, gain = b["plan"], b["gain"]
    D, S, M, X, R, NC, CW, HEADS = (z[n] for n in ("D", "S", "M", "X", "R", "NC", "CW", "HEADS"))
    first = [sum(HEADS[:c]) for c in range(NC)]
    wide = [count * HS for count in HEADS]
    CAP, CP, RB, RP, PX, DM = (z[n] for n in ("CAP", "CP", "RB", "RP", "PX", "DM"))
    d, s, m = lax.axis_index("dp"), lax.axis_index("seq"), lax.axis_index("mp")
    xi, co = s // 2, s % 2
    sent = []

    def remote(src, dst, ss, rs, **where):
        return pltpu.make_async_remote_copy(
            src_ref=src, dst_ref=dst, send_sem=ss, recv_sem=rs, device_id=where, device_id_type=MESH
        )

    def when(cond, act):
        if cond is None:
            act()
        else:
            pl.when(cond)(act)

    def go(copy, cond=None):
        when(cond, copy.start)
        sent.append((cond, copy))

    barrier = pltpu.get_barrier_semaphore()
    peers = 0

    def greet(**where):
        pl.semaphore_signal(barrier, inc=1, device_id=where, device_id_type=MESH)

    sources = (
        (plan_in, plan),
        (k_in, b["x"].at[K]),
        (v_in, b["x"].at[V]),
        (g_in, b["g"].at[m]),
        (seg_in, b["segi"]),
        (q_in, b["x"].at[Q]),
        (gain_in, gain),
    )
    loads = [pltpu.make_async_copy(a, c, b["in_s"].at[i]) for i, (a, c) in enumerate(sources)]
    for load in loads:
        load.start()
    w_loads = [
        pltpu.make_async_copy(
            w_in.at[pl.ds(first[c] * HS, wide[c]), :], b["w"].at[c, pl.ds(0, wide[c])], b["w_s"].at[c]
        )
        for c in range(NC)
    ]

    def fetch():
        for load in w_loads:
            load.start()

    if CP > CAP:
        b["arr"][:, :, :, CAP:CP, :] = jnp.zeros((3, NC, D, CP - CAP, CW), BF16)

    b["seg"][...] = jnp.full(b["seg"].shape, -1.0, F32)

    for t in range(D):
        for cc in range(2):
            if t or cc:
                greet(dp=lax.rem(d + t, D), seq=xi * 2 + (co + cc) % 2, mp=m)
                peers += 1
    for t in range(1, X):
        for cc in range(2):
            greet(dp=d, seq=lax.rem(xi + t, X) * 2 + cc, mp=m)
            peers += 1
    for t in range(1, M):
        greet(dp=d, seq=s, mp=lax.rem(m + t, M))
        peers += 1

    loads[0].wait()
    slot = lax.broadcasted_iota(jnp.int32, (D * CP, R), 0)
    row = lax.broadcasted_iota(jnp.int32, (D * CP, R), 1)
    start = jnp.int32(0)
    hot = jnp.zeros((D * CP, R), F32)
    for j in range(D):
        inside = (slot >= j * CP) & (slot < j * CP + CAP) & (row - start == slot - j * CP)
        hot = jnp.where(inside, 1.0, hot)
        start = start + plan[d, j]
    b["sel"][...] = hot.astype(BF16)
    slot = lax.broadcasted_iota(jnp.int32, (R, D * CP), 1)
    row = lax.broadcasted_iota(jnp.int32, (R, D * CP), 0)
    start = jnp.int32(0)
    hot = jnp.zeros((R, D * CP), F32)
    for i in range(D):
        count = plan[i, d]
        at = slot - i * CP
        inside = (at >= 0) & (at < CP) & (at == row - start) & (row - start < count)
        hot = jnp.where(inside, 1.0, hot)
        start = start + count
    b["pick"][...] = hot.astype(BF16)

    pl.semaphore_wait(barrier, peers)

    loads[3].wait()
    y_copies = []
    for t in range(1, M):
        c = remote(
            b["g"].at[m], b["g"].at[m], b["y_ss"].at[t - 1], b["y_rs"].at[t - 1], mp=lax.rem(m + t, M)
        )
        go(c)
        y_copies.append(c)
    loads[4].wait()
    b["seg"][0] = jnp.broadcast_to(b["segi"][...].astype(F32), (8, R))
    after, before = {}, {}
    for t in range(1, S):
        near, far = 2 * t - 1, 2 * t
        after[t] = remote(
            b["seg"].at[0], b["seg"].at[near], b["sg_ss"].at[near - 1], b["sg_rs"].at[near - 1], seq=lax.rem(s + t, S)
        )
        before[t] = remote(
            b["seg"].at[0], b["seg"].at[far], b["sg_ss"].at[far - 1], b["sg_rs"].at[far - 1], seq=lax.rem(s + S - t, S)
        )
        go(after[t], s + t < S)
        go(before[t], s - t >= 0)

    r_copies = {}

    waited = set()

    def pack(a, c):
        if a not in waited:
            waited.add(a)
            loads[(1, 2, 5)[a]].wait()
        at = first[c] * HS
        packed = mm(b["sel"][...], b["x"][a, :, at : at + wide[c]], 1, 0).astype(BF16)
        b["snd"][a, c, :, :, : wide[c]] = packed.reshape(D, CP, wide[c])
        b["arr"][a, c, d, :, : wide[c]] = b["snd"][a, c, d, :, : wide[c]]

    def send(a, c):
        for t in range(1, D):
            to = lax.rem(d + t, D)
            copy = remote(
                b["snd"].at[a, c, to, pl.ds(0, CAP), pl.ds(0, wide[c])],
                b["arr"].at[a, c, d, pl.ds(0, CAP), pl.ds(0, wide[c])],
                b["r_ss"].at[a, c, t],
                b["r_rs"].at[a, c, t],
                dp=to,
            )
            go(copy)
            r_copies[a, c, t] = copy

    def masks():
        for t in range(1, S):
            pl.when(s - t >= 0)(after[t].wait_recv)
            pl.when(s + t < S)(before[t].wait_recv)
        across = jnp.broadcast_to(b["seg"][0][0:1, :], (R, R))
        down = jnp.transpose(across)
        t_at = lax.broadcasted_iota(jnp.int32, (R, R), 0)
        u_at = lax.broadcasted_iota(jnp.int32, (R, R), 1)
        b["doc"][...] = jnp.where((u_at <= t_at) & (across == down), 1.0, 0.0)
        own_last = b["seg"][0][0:1, R - 1 : R]
        own_first = b["seg"][0][0:1, 0:1]
        last_before = b["seg"][1][0:1, R - 1 : R]
        first_after = b["seg"][2][0:1, 0:1]
        for i, value in ((TAIL, own_last), (HEAD, own_first), (CAR, last_before), (REV, first_after)):
            b["mk"][i] = jnp.where(down == jnp.broadcast_to(value, (R, R)), 1.0, 0.0).astype(BF16)
        for t in range(1, S):
            last_then = b["seg"][2 * t - 1][0:1, R - 1 : R]
            first_then = b["seg"][2 * t][0:1, 0:1]
            b["jn"][2 * t - 2] = jnp.broadcast_to(jnp.where(last_then == last_before, 1.0, 0.0), (8, R))
            b["jn"][2 * t - 1] = jnp.broadcast_to(jnp.where(first_then == first_after, 1.0, 0.0), (8, R))

    px, off = m // PX, pl.multiple_of((m % PX) * RP, RP)
    g_copies = []

    def turn():
        for c in y_copies:
            c.wait_recv()
        for i in range(M):
            for j in range(DM // HS):
                b["gt"][pl.ds(i * DM + j * HS, HS), :] = jnp.transpose(b["g"][i, :, j * HS : (j + 1) * HS])

    def terms():
        for t in range(D):
            for cc in range(2):
                to, core = lax.rem(d + t, D), (co + cc) % 2
                at = pl.multiple_of(((to * X + px) * 2 + core) * RB + off, RP)
                if t == 0 and cc == 0:
                    b["gz"][d, co, px, pl.ds(off, RP), :] = b["gt"][pl.ds(at, RP), :]
                    continue
                copy = remote(
                    b["gt"].at[pl.ds(at, RP), :],
                    b["gz"].at[d, co, px, pl.ds(off, RP), :],
                    b["g_ss"].at[t * 2 + cc],
                    b["g_rs"].at[t * 2 + cc],
                    dp=to,
                    seq=xi * 2 + core,
                )
                go(copy)
                g_copies.append(copy)

    def grow(c):
        w_loads[c].wait()
        total = mm(b["g"][0], b["w"][c, : wide[c], 0:DM], 1, 1)
        for i in range(1, M):
            total = total + mm(b["g"][i], b["w"][c, : wide[c], i * DM : (i + 1) * DM], 1, 1)
        b["dn"][c, :, : wide[c]] = total

    def place(a, c):
        for t in range(1, D):
            r_copies[a, c, t].wait_recv()
        parts = b["arr"][a, c, :, :, : wide[c]].reshape(D * CP, wide[c])
        b["f"][a, c, :, : wide[c]] = mm(b["pick"][...], parts, 1, 0).astype(BF16)

    s_copies, v_copies = {}, {}

    def part(ref, c, *at):
        return ref.at[(c, *at, slice(None), pl.ds(0, wide[c]))]

    def keep(c):
        place(K, c)
        place(V, c)
        for h in range(HEADS[c]):
            cols = slice(h * HS, (h + 1) * HS)
            term = mm(b["f"][K, c, :, cols] * b["mk"][TAIL], b["f"][V, c, :, cols], 0, 0)
            b["ls"][c, :, cols] = term.astype(BF16)
        for t in range(1, S):
            copy = remote(
                part(b["ls"], c), part(b["sr"], c, t - 1), b["f_ss"].at[c, t - 1], b["f_rs"].at[c, t - 1], seq=lax.rem(s + t, S)
            )
            go(copy, s + t < S)
            s_copies[c, t] = copy

    def gather(c, copies, there, came, kept, side):
        for t in range(1, S):
            pl.when(there(t))(copies[c, t].wait_recv)
        b["tot"][...] = jnp.zeros_like(b["tot"])
        for t in range(1, S):

            @pl.when(there(t))
            def _(t=t):
                run = jnp.broadcast_to(b["jn"][2 * t - 2 + side][0:1, 0:1], (HS, wide[c]))
                b["tot"][:, : wide[c]] += came[c, t - 1, :, : wide[c]].astype(F32) * run

        kept[c] = b["tot"][...].astype(BF16)

    def earlier(c):
        gather(c, s_copies, lambda t: s - t >= 0, b["sr"], b["st"], 0)

    def later(c):
        gather(c, v_copies, lambda t: s + t < S, b["rr"], b["rst"], 1)

    def spread(c, origin, right, left):
        block = part(b["nb"], c, origin, co)
        if right is not None:
            go(remote(block, block, b["nr_ss"].at[c, origin], b["n_rs"].at[c, origin], dp=jnp.minimum(d + 1, D - 1)), right)
        if left is not None:
            go(remote(block, block, b["nl_ss"].at[c, origin], b["n_rs"].at[c, origin], dp=jnp.maximum(d - 1, 0)), left)

    def share(c, origin, cond):
        block = part(b["nb"], c, origin, co)
        go(remote(block, block, b["p_ss"].at[c, origin], b["p_rs"].at[c, origin], seq=xi * 2 + 1 - co), cond)

    loads[6].wait()

    def forward(c):
        place(Q, c)
        earlier(c)
        for h in range(HEADS[c]):
            cols = slice(h * HS, (h + 1) * HS)
            q, k, v = (b["f"][a, c, :, cols] for a in (Q, K, V))
            p = (mm(q, k, 1, 1) * b["doc"][...]).astype(BF16)
            b["pm"][c, :, cols] = p
            both = jnp.concatenate([p, q * b["mk"][CAR]], axis=1)
            attn = mm(both, jnp.concatenate([v, b["st"][c, :, cols]], axis=0), 1, 0)
            gain_h = gain[:, (first[c] + h) * HS : (first[c] + h + 1) * HS]
            scale = lax.rsqrt(jnp.mean(attn * attn, axis=-1, keepdims=True) + NORM_EPS)
            unit = attn * scale
            out = (unit * gain_h).astype(BF16)
            b["nb"][c, d, co, :, cols] = out
            normed_out[c, :, cols] = out
            g = b["dn"][c, :, cols] * gain_h
            d_attn = scale * (g - unit * jnp.mean(g * unit, axis=-1, keepdims=True))
            b["dh"][c, :, cols] = d_attn.astype(BF16)
        spread(c, d, d < D - 1, d > 0)
        share(c, d, None)
        for h in range(HEADS[c]):
            cols = slice(h * HS, (h + 1) * HS)
            term = mm(b["f"][Q, c, :, cols] * b["mk"][HEAD], b["dh"][c, :, cols], 0, 0)
            b["lr"][c, :, cols] = term.astype(BF16)
        for t in range(1, S):
            copy = remote(
                part(b["lr"], c), part(b["rr"], c, t - 1), b["v_ss"].at[c, t - 1], b["v_rs"].at[c, t - 1], seq=lax.rem(s + S - t, S)
            )
            go(copy, s - t >= 0)
            v_copies[c, t] = copy

    def arrived(c, origin):
        block = part(b["nb"], c, origin, co)
        remote(block, block, b["nr_ss"].at[c, origin], b["n_rs"].at[c, origin], dp=lax.rem(d + 1, D)).wait_recv()

    def relay(c, step):
        @pl.when(d - step >= 0)
        def _():
            arrived(c, d - step)

        spread(c, jnp.maximum(d - step, 0), (d - step >= 0) & (d < D - 1), None)
        share(c, jnp.maximum(d - step, 0), d - step >= 0)

        @pl.when(d + step < D)
        def _():
            arrived(c, d + step)

        spread(c, jnp.minimum(d + step, D - 1), None, (d + step < D) & (d > 0))
        share(c, jnp.minimum(d + step, D - 1), d + step < D)

    def backward(c):
        later(c)
        for h in range(HEADS[c]):
            cols = slice(h * HS, (h + 1) * HS)
            q, k, v = (b["f"][a, c, :, cols] for a in (Q, K, V))
            dh, p = b["dh"][c, :, cols], b["pm"][c, :, cols]
            st, rst = b["st"][c, :, cols], b["rst"][c, :, cols]
            dp = (mm(dh, v, 1, 1) * b["doc"][...]).astype(BF16)
            rev = b["mk"][REV]
            grads_out[0, c, :, cols] = (mm(dp, k, 1, 0) + mm(dh * b["mk"][CAR], st, 1, 1)).astype(BF16)
            grads_out[1, c, :, cols] = (mm(dp, q, 0, 0) + mm(v * rev, rst, 1, 1)).astype(BF16)
            grads_out[2, c, :, cols] = (mm(p, dh, 0, 0) + mm(k * rev, rst, 1, 0)).astype(BF16)

    def add(c, origin, t, cols, fresh=False):
        to = lax.rem(xi + t, X)
        left = jnp.concatenate([b["gz"][origin, 0, to], b["gz"][origin, 1, to]], axis=1)
        right = b["nb"][c, origin, :, :, cols].reshape(2 * R, cols.stop - cols.start)
        term = mm(left, right, 1, 0)
        b["acc"][c, t, :, cols] = term if fresh else b["acc"][c, t, :, cols] + term

    def pieces(c):
        half = wide[c] // 2
        return (slice(0, half), slice(half, wide[c])) if wide[c] > 2 * HS and half % HS == 0 else (slice(0, wide[c]),)

    def paired(c, origin):
        block = part(b["nb"], c, origin, 1 - co)
        remote(block, block, b["p_ss"].at[c, origin], b["p_rs"].at[c, origin], seq=xi * 2 + 1 - co).wait_recv()

    def each(step, act):
        if step == 0:
            act(d)
            return
        pl.when(d - step >= 0)(lambda: act(d - step))
        pl.when(d + step < D)(lambda: act(d + step))

    def absorb(c, step):
        def one(origin):
            paired(c, origin)
            for t in range(X):
                add(c, origin, t, slice(0, wide[c]), fresh=step == 0)

        each(step, one)

    x_copies = {}

    def close(c, step):
        each(step, lambda origin: paired(c, origin))
        for t in list(range(1, X)) + [0]:
            for i, cols in enumerate(pieces(c)):
                each(step, lambda origin: add(c, origin, t, cols, fresh=step == 0))
                if t == 0:
                    continue
                b["xs"][c, t - 1, :, cols] = b["acc"][c, t, :, cols].astype(BF16)
                some = pl.ds(cols.start, cols.stop - cols.start)
                copy = remote(
                    b["xs"].at[c, t - 1, :, some],
                    b["xr"].at[c, t - 1, :, some],
                    b["x_ss"].at[c, t - 1, i],
                    b["x_rs"].at[c, t - 1, i],
                    seq=lax.rem(xi + t, X) * 2 + co,
                )
                go(copy)
                x_copies[c, t, i] = copy

    def settle(c):
        for i, cols in enumerate(pieces(c)):
            total = b["acc"][c, 0, :, cols]
            for t in range(1, X):
                x_copies[c, t, i].wait_recv()
                total = total + b["xr"][c, t - 1, :, cols].astype(F32)
            wg_out[c, :, cols] = total

    b_copies = []

    def double():
        for copy in g_copies:
            copy.wait_recv()
        mine = b["gz"].at[:, :, px, pl.ds(off, RP), :]
        for t in range(1, M):
            copy = remote(mine, mine, b["b_ss"].at[t - 1], b["b_rs"].at[t - 1], mp=lax.rem(m + t, M))
            go(copy)
            b_copies.append(copy)

    def doubled():
        for copy in b_copies:
            copy.wait_recv()

    last = D - 1
    acts = dict(
        pack=pack,
        send=send,
        fetch=fetch,
        masks=masks,
        turn=turn,
        terms=terms,
        grow=grow,
        keep=keep,
        forward=forward,
        relay=relay,
        backward=backward,
        double=double,
        doubled=doubled,
        absorb=absorb,
        close=lambda c: close(c, last),
        settle=settle,
    )
    for name, *args in order(NC, D):
        acts[name](*args)
    for cond, copy in sent:
        when(cond, copy.wait_send)


def write_body(heads, normed, grads, wg, *refs):
    outs, sem = refs[:5], refs[5]
    copies = []
    for c, count in enumerate(heads):
        cols, some = pl.ds(sum(heads[:c]) * HS, count * HS), pl.ds(0, count * HS)
        parts = (normed.at[c], grads.at[0, c], grads.at[1, c], grads.at[2, c], wg.at[c])
        for i, (part, out) in enumerate(zip(parts, outs)):
            copies.append(pltpu.make_async_copy(part.at[:, some], out.at[:, cols], sem.at[c, i]))
    for copy in copies:
        copy.start()
    for copy in copies:
        copy.wait()


def solution(mesh):
    def local(queries, key_rows, value_rows, row_plan, segments, norm_gain, out_weight, out_grad):
        rows, width = queries.shape
        z = plan_sizes(mesh, rows, width, out_grad.shape[1])
        scratch = scratch_of(z)
        chunks, span = z["NC"], z["CW"]
        anywhere = pl.BlockSpec(memory_space=pl.ANY)
        vmem = pl.BlockSpec(memory_space=pltpu.VMEM)
        operands = (
            row_plan,
            segments,
            norm_gain.reshape(1, width),
            queries,
            key_rows,
            value_rows,
            out_weight,
            out_grad,
        )
        kept = pl.pallas_call(
            functools.partial(whole_body, z, tuple(scratch)),
            out_shape=[
                pltpu.VMEM((chunks, rows, span), BF16),
                pltpu.VMEM((3, chunks, rows, span), BF16),
                pltpu.VMEM((chunks, z["RB"], span), F32),
            ],
            in_specs=[pl.BlockSpec(memory_space=pltpu.HBM)] * 8,
            out_specs=[vmem] * 3,
            scratch_shapes=list(scratch.values()),
            compiler_params=pltpu.CompilerParams(
                collective_id=0, has_side_effects=True, vmem_limit_bytes=50 * 1024 * 1024
            ),
        )(*(pltpu.with_memory_space_constraint(a, pltpu.HBM) for a in operands))
        half = jax.ShapeDtypeStruct((rows, width), BF16)
        return pl.pallas_call(
            functools.partial(write_body, z["HEADS"]),
            out_shape=[half, half, half, half, jax.ShapeDtypeStruct((z["RB"], width), F32)],
            in_specs=[anywhere] * 3,
            out_specs=[anywhere] * 5,
            scratch_shapes=[pltpu.SemaphoreType.DMA((chunks, 5))],
            compiler_params=pltpu.CompilerParams(vmem_limit_bytes=4 * 1024 * 1024),
        )(*kept)

    placed = (
        P(("dp", "seq"), "mp"),
        P(("dp", "seq"), "mp"),
        P(("dp", "seq"), "mp"),
        P(),
        P("dp", "seq"),
        P("mp"),
        P("mp", None),
        P(("dp", "seq"), "mp"),
    )
    return jax.shard_map(
        local, mesh=mesh, in_specs=placed, out_specs=(P(("dp", "seq"), "mp"),) * 5, check_vma=False
    )
```

```python
import functools

import jax
import jax.numpy as jnp
from jax import lax
from jax.experimental import pallas as pl
from jax.experimental.pallas import tpu as pltpu
from jax.sharding import PartitionSpec as P

HS = 128
NORM_EPS = 1e-06
F32 = jnp.float32
BF16 = jnp.bfloat16
MESH = pl.DeviceIdType.MESH
K, V, Q = 0, 1, 2
SPAN = 4
TERMS = 1
STEP = 2


def mm(a, b, ca, cb):
    return lax.dot_general(a, b, (((ca,), (cb,)), ((), ())), preferred_element_type=F32)


def plan_sizes(mesh, rows, width, out_half):
    groups, shards, splits = mesh.shape["dp"], mesh.shape["seq"], mesh.shape["mp"]
    z = {}
    z["D"], z["S"], z["M"], z["X"] = groups, shards, splits, shards // 2
    z["R"], z["W"], z["DM"] = rows, width, out_half
    z["DOUT"] = out_half * splits
    heads = width // HS
    full, rest = divmod(heads, SPAN)
    z["HEADS"] = [SPAN] * full + [rest] * (rest > 0)
    z["NC"] = len(z["HEADS"])
    z["CW"] = max(z["HEADS"]) * HS
    z["CAP"] = rows // min(groups, 8) + rows // 16
    z["CP"] = -(-z["CAP"] // 16) * 16
    z["RB"] = z["DOUT"] // (groups * shards)
    z["PX"] = splits // z["X"]
    z["RP"] = z["RB"] // z["PX"]
    return z


def scratch_of(z):
    D, M, X, R, W, NC, CW = (z[n] for n in ("D", "M", "X", "R", "W", "NC", "CW"))
    XO, SO = max(1, X - 1), max(1, z["S"] - 1)
    vm = pltpu.VMEM
    dma = pltpu.SemaphoreType.DMA
    return dict(
        x=vm((3, R, W), BF16),
        snd=vm((3, NC, D, z["CP"], CW), BF16),
        arr=vm((3, NC, D, z["CP"], CW), BF16),
        f=vm((3, NC, R, CW), BF16),
        w=vm((NC, CW, z["DOUT"]), BF16),
        g=vm((M, R, z["DM"]), BF16),
        gt=vm((z["DOUT"], R), BF16),
        gz=vm((D, 2, X, z["RB"], R), BF16),
        plan=pltpu.SMEM((D, D), jnp.int32),
        segi=vm((1, R), jnp.int32),
        gain=vm((1, W), F32),
        dn=vm((NC, R, CW), F32),
        pm=vm((NC, R, CW), BF16),
        tot=vm((HS, CW), F32),
        ls=vm((NC, HS, CW), BF16),
        sr=vm((NC, SO, HS, CW), BF16),
        st=vm((NC, HS, CW), BF16),
        lr=vm((NC, HS, CW), BF16),
        rr=vm((NC, SO, HS, CW), BF16),
        rst=vm((NC, HS, CW), BF16),
        dh=vm((NC, R, CW), BF16),
        nb=vm((NC, D, 2, R, CW), BF16),
        acc=vm((NC, X, z["RB"], CW), F32),
        xs=vm((NC, XO, z["RB"], CW), BF16),
        xr=vm((NC, XO, z["RB"], CW), BF16),
        seg=vm((2 * SO + 1, 8, R), F32),
        doc=vm((R, R), F32),
        mk=vm((4, R, R), BF16),
        jn=vm((2 * SO, 8, R), F32),
        sel=vm((D * z["CP"], R), BF16),
        pick=vm((R, D * z["CP"]), BF16),
        in_s=dma((4,)),
        h_s=dma((3, NC)),
        w_s=dma((NC,)),
        y_ss=dma((max(1, M - 1),)),
        y_rs=dma((max(1, M - 1),)),
        sg_ss=dma((2 * SO,)),
        sg_rs=dma((2 * SO,)),
        r_ss=dma((3, NC, D)),
        r_rs=dma((3, NC, D)),
        g_ss=dma((2 * D,)),
        g_rs=dma((2 * D,)),
        b_ss=dma((max(1, M - 1),)),
        b_rs=dma((max(1, M - 1),)),
        f_ss=dma((NC, SO)),
        f_rs=dma((NC, SO)),
        v_ss=dma((NC, SO)),
        v_rs=dma((NC, SO)),
        nr_ss=dma((NC, D)),
        nl_ss=dma((NC, D)),
        n_rs=dma((NC, D)),
        p_ss=dma((NC, D)),
        p_rs=dma((NC, D)),
        x_ss=dma((NC, XO, 2)),
        x_rs=dma((NC, XO, 2)),
    )


TAIL, HEAD, CAR, REV = 0, 1, 2, 3


def order(n, groups):
    last = groups - 1
    steps = []

    def do(name, *args):
        steps.append((name, *args))

    def rows(act, c, *names):
        for a in names if c < n else ():
            do(act, a, c)

    rows("pack", 0, K)
    rows("send", 0, K)
    rows("pack", 0, V)
    rows("send", 0, V)
    do("fetch")
    for c in range(2):
        rows("pack", c + 1, K, V)
        rows("send", c + 1, K, V)
        rows("pack", c, Q)
        rows("send", c, Q)
    do("masks")
    for c in range(2, n):
        rows("pack", c + 1, K, V)
        rows("pack", c, Q)
    do("turn")
    for c in range(min(2, n)):
        do("grow", c)
        do("keep", c)
    early = []
    left = [(STEP * k + c, c, k) for c in range(n) for k in range(1, last + 1)]
    for c in range(n):
        do("forward", c)
        if c == TERMS:
            do("terms")
        rows("send", c + 3, K, V)
        rows("send", c + 2, Q)
        if c + 2 < n:
            do("grow", c + 2)
        if 1 <= c < n - 1 and last > 1:
            do("relay", c - 1, 1)
            left.remove((STEP + c - 1, c - 1, 1))
            early.append((c - 1, 0))
        if c + 2 < n:
            do("keep", c + 2)
        if 2 <= c < n - 1:
            do("backward", c - 2)
    if n <= TERMS:
        do("terms")
    do("double")
    behind, closed, due, ready = list(range(max(0, n - 3), n)), [], early, False

    def finish(c):
        if ("doubled",) not in steps:
            do("doubled")
        for item in [item for item in due if item[0] == c]:
            do("absorb", *item)
            due.remove(item)
        do("close", c)
        closed.append(c)

    for _, c, k in sorted(left):
        if (c, k) == (n - 1, last):
            while behind:
                do("backward", behind.pop(0))
        do("relay", c, k)
        if (c, k) == (n - 2, 1):
            do("backward", behind.pop(0))
        if (c, k) == (n - 1, 1):
            if ("doubled",) not in steps:
                do("doubled")
            ready = True
        if k == 1:
            due.append((c, 0))
        else:
            due.append((c, k - 1))
        if ready:
            for item in [item for item in due if item[0] == due[0][0] and item[1] < last - 1][:2]:
                do("absorb", *item)
                due.remove(item)
        if (c, k) == (n - 1, last - 1) and behind:
            do("backward", behind.pop(0))
        if k == last:
            finish(c)
    if not last:
        due.extend((c, 0) for c in range(n))
        for c in range(n):
            finish(c)
    while behind:
        do("backward", behind.pop(0))
    for c in closed:
        do("settle", c)
    return steps


def whole_body(z, names, *refs):
    plan_in, seg_in, gain_in, q_in, k_in, v_in, w_in, g_in = refs[:8]
    normed_out, grads_out, wg_out = refs[8:11]
    b = dict(zip(names, refs[11:]))
    plan, gain = b["plan"], b["gain"]
    D, S, M, X, R, NC, CW, HEADS = (z[n] for n in ("D", "S", "M", "X", "R", "NC", "CW", "HEADS"))
    first = [sum(HEADS[:c]) for c in range(NC)]
    wide = [count * HS for count in HEADS]
    CAP, CP, RB, RP, PX, DM = (z[n] for n in ("CAP", "CP", "RB", "RP", "PX", "DM"))
    d, s, m = lax.axis_index("dp"), lax.axis_index("seq"), lax.axis_index("mp")
    xi, co = s // 2, s % 2
    sent = []

    def remote(src, dst, ss, rs, **where):
        return pltpu.make_async_remote_copy(
            src_ref=src, dst_ref=dst, send_sem=ss, recv_sem=rs, device_id=where, device_id_type=MESH
        )

    def when(cond, act):
        if cond is None:
            act()
        else:
            pl.when(cond)(act)

    def go(copy, cond=None):
        when(cond, copy.start)
        sent.append((cond, copy))

    barrier = pltpu.get_barrier_semaphore()
    peers = 0

    def greet(**where):
        pl.semaphore_signal(barrier, inc=1, device_id=where, device_id_type=MESH)

    sources = ((plan_in, plan), (g_in, b["g"].at[m]), (seg_in, b["segi"]), (gain_in, gain))
    loads = [pltpu.make_async_copy(a, c, b["in_s"].at[i]) for i, (a, c) in enumerate(sources)]
    h_loads = {}
    for c in range(NC):
        cols = pl.ds(first[c] * HS, wide[c])
        for a, whole in ((K, k_in), (V, v_in), (Q, q_in)):
            h_loads[a, c] = pltpu.make_async_copy(whole.at[:, cols], b["x"].at[a, :, cols], b["h_s"].at[a, c])
    loads[0].start()
    h_loads[K, 0].start()
    h_loads[V, 0].start()
    for load in loads[1:]:
        load.start()
    for at, load in h_loads.items():
        if at not in ((K, 0), (V, 0)):
            load.start()
    w_loads = [
        pltpu.make_async_copy(
            w_in.at[pl.ds(first[c] * HS, wide[c]), :], b["w"].at[c, pl.ds(0, wide[c])], b["w_s"].at[c]
        )
        for c in range(NC)
    ]

    def fetch():
        for load in w_loads:
            load.start()

    if CP > CAP:
        b["arr"][:, :, :, CAP:CP, :] = jnp.zeros((3, NC, D, CP - CAP, CW), BF16)

    b["seg"][...] = jnp.full(b["seg"].shape, -1.0, F32)

    for t in range(D):
        for cc in range(2):
            if t or cc:
                greet(dp=lax.rem(d + t, D), seq=xi * 2 + (co + cc) % 2, mp=m)
                peers += 1
    for t in range(1, X):
        for cc in range(2):
            greet(dp=d, seq=lax.rem(xi + t, X) * 2 + cc, mp=m)
            peers += 1
    for t in range(1, M):
        greet(dp=d, seq=s, mp=lax.rem(m + t, M))
        peers += 1

    loads[0].wait()
    slot = lax.broadcasted_iota(jnp.int32, (D * CP, R), 0)
    row = lax.broadcasted_iota(jnp.int32, (D * CP, R), 1)
    start = jnp.int32(0)
    hot = jnp.zeros((D * CP, R), F32)
    for j in range(D):
        inside = (slot >= j * CP) & (slot < j * CP + CAP) & (row - start == slot - j * CP)
        hot = jnp.where(inside, 1.0, hot)
        start = start + plan[d, j]
    b["sel"][...] = hot.astype(BF16)
    slot = lax.broadcasted_iota(jnp.int32, (R, D * CP), 1)
    row = lax.broadcasted_iota(jnp.int32, (R, D * CP), 0)
    start = jnp.int32(0)
    hot = jnp.zeros((R, D * CP), F32)
    for i in range(D):
        count = plan[i, d]
        at = slot - i * CP
        inside = (at >= 0) & (at < CP) & (at == row - start) & (row - start < count)
        hot = jnp.where(inside, 1.0, hot)
        start = start + count
    b["pick"][...] = hot.astype(BF16)

    pl.semaphore_wait(barrier, peers)

    loads[1].wait()
    y_copies = []
    for t in range(1, M):
        c = remote(
            b["g"].at[m], b["g"].at[m], b["y_ss"].at[t - 1], b["y_rs"].at[t - 1], mp=lax.rem(m + t, M)
        )
        go(c)
        y_copies.append(c)
    loads[2].wait()
    b["seg"][0] = jnp.broadcast_to(b["segi"][...].astype(F32), (8, R))
    after, before = {}, {}
    for t in range(1, S):
        near, far = 2 * t - 1, 2 * t
        after[t] = remote(
            b["seg"].at[0], b["seg"].at[near], b["sg_ss"].at[near - 1], b["sg_rs"].at[near - 1], seq=lax.rem(s + t, S)
        )
        before[t] = remote(
            b["seg"].at[0], b["seg"].at[far], b["sg_ss"].at[far - 1], b["sg_rs"].at[far - 1], seq=lax.rem(s + S - t, S)
        )
        go(after[t], s + t < S)
        go(before[t], s - t >= 0)

    r_copies = {}

    def pack(a, c):
        h_loads[a, c].wait()
        at = first[c] * HS
        packed = mm(b["sel"][...], b["x"][a, :, at : at + wide[c]], 1, 0).astype(BF16)
        b["snd"][a, c, :, :, : wide[c]] = packed.reshape(D, CP, wide[c])
        b["arr"][a, c, d, :, : wide[c]] = b["snd"][a, c, d, :, : wide[c]]

    def send(a, c):
        for t in range(1, D):
            to = lax.rem(d + t, D)
            copy = remote(
                b["snd"].at[a, c, to, pl.ds(0, CAP), pl.ds(0, wide[c])],
                b["arr"].at[a, c, d, pl.ds(0, CAP), pl.ds(0, wide[c])],
                b["r_ss"].at[a, c, t],
                b["r_rs"].at[a, c, t],
                dp=to,
            )
            go(copy)
            r_copies[a, c, t] = copy

    def masks():
        for t in range(1, S):
            pl.when(s - t >= 0)(after[t].wait_recv)
            pl.when(s + t < S)(before[t].wait_recv)
        across = jnp.broadcast_to(b["seg"][0][0:1, :], (R, R))
        down = jnp.transpose(across)
        t_at = lax.broadcasted_iota(jnp.int32, (R, R), 0)
        u_at = lax.broadcasted_iota(jnp.int32, (R, R), 1)
        b["doc"][...] = jnp.where((u_at <= t_at) & (across == down), 1.0, 0.0)
        own_last = b["seg"][0][0:1, R - 1 : R]
        own_first = b["seg"][0][0:1, 0:1]
        last_before = b["seg"][1][0:1, R - 1 : R]
        first_after = b["seg"][2][0:1, 0:1]
        for i, value in ((TAIL, own_last), (HEAD, own_first), (CAR, last_before), (REV, first_after)):
            b["mk"][i] = jnp.where(down == jnp.broadcast_to(value, (R, R)), 1.0, 0.0).astype(BF16)
        for t in range(1, S):
            last_then = b["seg"][2 * t - 1][0:1, R - 1 : R]
            first_then = b["seg"][2 * t][0:1, 0:1]
            b["jn"][2 * t - 2] = jnp.broadcast_to(jnp.where(last_then == last_before, 1.0, 0.0), (8, R))
            b["jn"][2 * t - 1] = jnp.broadcast_to(jnp.where(first_then == first_after, 1.0, 0.0), (8, R))

    px, off = m // PX, pl.multiple_of((m % PX) * RP, RP)
    g_copies = []

    def turn():
        for c in y_copies:
            c.wait_recv()
        for i in range(M):
            for j in range(DM // HS):
                b["gt"][pl.ds(i * DM + j * HS, HS), :] = jnp.transpose(b["g"][i, :, j * HS : (j + 1) * HS])

    def terms():
        for t in range(D):
            for cc in range(2):
                to, core = lax.rem(d + t, D), (co + cc) % 2
                at = pl.multiple_of(((to * X + px) * 2 + core) * RB + off, RP)
                if t == 0 and cc == 0:
                    b["gz"][d, co, px, pl.ds(off, RP), :] = b["gt"][pl.ds(at, RP), :]
                    continue
                copy = remote(
                    b["gt"].at[pl.ds(at, RP), :],
                    b["gz"].at[d, co, px, pl.ds(off, RP), :],
                    b["g_ss"].at[t * 2 + cc],
                    b["g_rs"].at[t * 2 + cc],
                    dp=to,
                    seq=xi * 2 + core,
                )
                go(copy)
                g_copies.append(copy)

    def grow(c):
        w_loads[c].wait()
        total = mm(b["g"][0], b["w"][c, : wide[c], 0:DM], 1, 1)
        for i in range(1, M):
            total = total + mm(b["g"][i], b["w"][c, : wide[c], i * DM : (i + 1) * DM], 1, 1)
        b["dn"][c, :, : wide[c]] = total

    def place(a, c):
        for t in range(1, D):
            r_copies[a, c, t].wait_recv()
        parts = b["arr"][a, c, :, :, : wide[c]].reshape(D * CP, wide[c])
        b["f"][a, c, :, : wide[c]] = mm(b["pick"][...], parts, 1, 0).astype(BF16)

    s_copies, v_copies = {}, {}

    def part(ref, c, *at):
        return ref.at[(c, *at, slice(None), pl.ds(0, wide[c]))]

    def keep(c):
        place(K, c)
        place(V, c)
        for h in range(HEADS[c]):
            cols = slice(h * HS, (h + 1) * HS)
            term = mm(b["f"][K, c, :, cols] * b["mk"][TAIL], b["f"][V, c, :, cols], 0, 0)
            b["ls"][c, :, cols] = term.astype(BF16)
        for t in range(1, S):
            copy = remote(
                part(b["ls"], c), part(b["sr"], c, t - 1), b["f_ss"].at[c, t - 1], b["f_rs"].at[c, t - 1], seq=lax.rem(s + t, S)
            )
            go(copy, s + t < S)
            s_copies[c, t] = copy

    def gather(c, copies, there, came, kept, side):
        for t in range(1, S):
            pl.when(there(t))(copies[c, t].wait_recv)
        b["tot"][...] = jnp.zeros_like(b["tot"])
        for t in range(1, S):

            @pl.when(there(t))
            def _(t=t):
                run = jnp.broadcast_to(b["jn"][2 * t - 2 + side][0:1, 0:1], (HS, wide[c]))
                b["tot"][:, : wide[c]] += came[c, t - 1, :, : wide[c]].astype(F32) * run

        kept[c] = b["tot"][...].astype(BF16)

    def earlier(c):
        gather(c, s_copies, lambda t: s - t >= 0, b["sr"], b["st"], 0)

    def later(c):
        gather(c, v_copies, lambda t: s + t < S, b["rr"], b["rst"], 1)

    def spread(c, origin, right, left):
        block = part(b["nb"], c, origin, co)
        if right is not None:
            go(remote(block, block, b["nr_ss"].at[c, origin], b["n_rs"].at[c, origin], dp=jnp.minimum(d + 1, D - 1)), right)
        if left is not None:
            go(remote(block, block, b["nl_ss"].at[c, origin], b["n_rs"].at[c, origin], dp=jnp.maximum(d - 1, 0)), left)

    def share(c, origin, cond):
        block = part(b["nb"], c, origin, co)
        go(remote(block, block, b["p_ss"].at[c, origin], b["p_rs"].at[c, origin], seq=xi * 2 + 1 - co), cond)

    loads[3].wait()

    def forward(c):
        place(Q, c)
        earlier(c)
        held = []
        for h in range(HEADS[c]):
            cols = slice(h * HS, (h + 1) * HS)
            q, k, v = (b["f"][a, c, :, cols] for a in (Q, K, V))
            p = (mm(q, k, 1, 1) * b["doc"][...]).astype(BF16)
            b["pm"][c, :, cols] = p
            both = jnp.concatenate([p, q * b["mk"][CAR]], axis=1)
            attn = mm(both, jnp.concatenate([v, b["st"][c, :, cols]], axis=0), 1, 0)
            gain_h = gain[:, (first[c] + h) * HS : (first[c] + h + 1) * HS]
            scale = lax.rsqrt(jnp.mean(attn * attn, axis=-1, keepdims=True) + NORM_EPS)
            unit = attn * scale
            out = (unit * gain_h).astype(BF16)
            b["nb"][c, d, co, :, cols] = out
            normed_out[c, :, cols] = out
            held.append((gain_h, scale, unit))
        spread(c, d, d < D - 1, d > 0)
        share(c, d, None)
        for h in range(HEADS[c]):
            cols = slice(h * HS, (h + 1) * HS)
            gain_h, scale, unit = held[h]
            g = b["dn"][c, :, cols] * gain_h
            d_attn = scale * (g - unit * jnp.mean(g * unit, axis=-1, keepdims=True))
            b["dh"][c, :, cols] = d_attn.astype(BF16)
        for h in range(HEADS[c]):
            cols = slice(h * HS, (h + 1) * HS)
            term = mm(b["f"][Q, c, :, cols] * b["mk"][HEAD], b["dh"][c, :, cols], 0, 0)
            b["lr"][c, :, cols] = term.astype(BF16)
        for t in range(1, S):
            copy = remote(
                part(b["lr"], c), part(b["rr"], c, t - 1), b["v_ss"].at[c, t - 1], b["v_rs"].at[c, t - 1], seq=lax.rem(s + S - t, S)
            )
            go(copy, s - t >= 0)
            v_copies[c, t] = copy

    def arrived(c, origin):
        block = part(b["nb"], c, origin, co)
        remote(block, block, b["nr_ss"].at[c, origin], b["n_rs"].at[c, origin], dp=lax.rem(d + 1, D)).wait_recv()

    def from_left(c, step, cond):
        cond = cond & (d - step >= 0)
        origin = jnp.maximum(d - step, 0)
        pl.when(cond)(lambda: arrived(c, d - step))
        spread(c, origin, cond & (d < D - 1), None)
        share(c, origin, cond)

    def from_right(c, step, cond):
        cond = cond & (d + step < D)
        origin = jnp.minimum(d + step, D - 1)
        pl.when(cond)(lambda: arrived(c, d + step))
        spread(c, origin, None, cond & (d > 0))
        share(c, origin, cond)

    low = d < D // 2
    high = d >= D // 2

    def inward(c, step):
        from_left(c, step, low)
        from_right(c, step, high)

    def outward(c, step):
        from_right(c, step, low)
        from_left(c, step, high)

    def relay(c, step):
        if step < (D + 1) // 2:
            inward(c, step)
        outward(c, step)

    def backward(c):
        later(c)
        for h in range(HEADS[c]):
            cols = slice(h * HS, (h + 1) * HS)
            q, k, v = (b["f"][a, c, :, cols] for a in (Q, K, V))
            dh, p = b["dh"][c, :, cols], b["pm"][c, :, cols]
            st, rst = b["st"][c, :, cols], b["rst"][c, :, cols]
            dp = (mm(dh, v, 1, 1) * b["doc"][...]).astype(BF16)
            rev = b["mk"][REV]
            grads_out[0, c, :, cols] = (mm(dp, k, 1, 0) + mm(dh * b["mk"][CAR], st, 1, 1)).astype(BF16)
            grads_out[1, c, :, cols] = (mm(dp, q, 0, 0) + mm(v * rev, rst, 1, 1)).astype(BF16)
            grads_out[2, c, :, cols] = (mm(p, dh, 0, 0) + mm(k * rev, rst, 1, 0)).astype(BF16)

    def add(c, origin, t, cols, fresh=False):
        to = lax.rem(xi + t, X)
        left = jnp.concatenate([b["gz"][origin, 0, to], b["gz"][origin, 1, to]], axis=1)
        right = b["nb"][c, origin, :, :, cols].reshape(2 * R, cols.stop - cols.start)
        term = mm(left, right, 1, 0)
        b["acc"][c, t, :, cols] = term if fresh else b["acc"][c, t, :, cols] + term

    def pieces(c):
        half = wide[c] // 2
        return (slice(0, half), slice(half, wide[c])) if wide[c] > 2 * HS and half % HS == 0 else (slice(0, wide[c]),)

    def paired(c, origin):
        block = part(b["nb"], c, origin, 1 - co)
        remote(block, block, b["p_ss"].at[c, origin], b["p_rs"].at[c, origin], seq=xi * 2 + 1 - co).wait_recv()

    def each(step, act):
        if step == 0:
            act(d)
            return
        pl.when(d - step >= 0)(lambda: act(d - step))
        pl.when(d + step < D)(lambda: act(d + step))

    def absorb(c, step):
        def one(origin):
            paired(c, origin)
            for t in range(X):
                add(c, origin, t, slice(0, wide[c]), fresh=step == 0)

        each(step, one)

    x_copies = {}

    def close(c, step):
        each(step, lambda origin: paired(c, origin))
        for t in list(range(1, X)) + [0]:
            for i, cols in enumerate(pieces(c)):
                each(step, lambda origin: add(c, origin, t, cols, fresh=step == 0))
                if t == 0:
                    continue
                b["xs"][c, t - 1, :, cols] = b["acc"][c, t, :, cols].astype(BF16)
                some = pl.ds(cols.start, cols.stop - cols.start)
                copy = remote(
                    b["xs"].at[c, t - 1, :, some],
                    b["xr"].at[c, t - 1, :, some],
                    b["x_ss"].at[c, t - 1, i],
                    b["x_rs"].at[c, t - 1, i],
                    seq=lax.rem(xi + t, X) * 2 + co,
                )
                go(copy)
                x_copies[c, t, i] = copy

    def settle(c):
        for i, cols in enumerate(pieces(c)):
            total = b["acc"][c, 0, :, cols]
            for t in range(1, X):
                x_copies[c, t, i].wait_recv()
                total = total + b["xr"][c, t - 1, :, cols].astype(F32)
            wg_out[c, :, cols] = total

    b_copies = []

    def double():
        for copy in g_copies:
            copy.wait_recv()
        mine = b["gz"].at[:, :, px, pl.ds(off, RP), :]
        for t in range(1, M):
            copy = remote(mine, mine, b["b_ss"].at[t - 1], b["b_rs"].at[t - 1], mp=lax.rem(m + t, M))
            go(copy)
            b_copies.append(copy)

    def doubled():
        for copy in b_copies:
            copy.wait_recv()

    last = D - 1
    acts = dict(
        pack=pack,
        send=send,
        fetch=fetch,
        masks=masks,
        turn=turn,
        terms=terms,
        grow=grow,
        keep=keep,
        forward=forward,
        relay=relay,
        backward=backward,
        double=double,
        doubled=doubled,
        absorb=absorb,
        close=lambda c: close(c, last),
        settle=settle,
    )
    for name, *args in order(NC, D):
        acts[name](*args)
    for cond, copy in sent:
        when(cond, copy.wait_send)


def write_body(heads, normed, grads, wg, *refs):
    outs, sem = refs[:5], refs[5]
    copies = []
    for c, count in enumerate(heads):
        cols, some = pl.ds(sum(heads[:c]) * HS, count * HS), pl.ds(0, count * HS)
        parts = (normed.at[c], grads.at[0, c], grads.at[1, c], grads.at[2, c], wg.at[c])
        for i, (part, out) in enumerate(zip(parts, outs)):
            copies.append(pltpu.make_async_copy(part.at[:, some], out.at[:, cols], sem.at[c, i]))
    for copy in copies:
        copy.start()
    for copy in copies:
        copy.wait()


def solution(mesh):
    def local(queries, key_rows, value_rows, row_plan, segments, norm_gain, out_weight, out_grad):
        rows, width = queries.shape
        z = plan_sizes(mesh, rows, width, out_grad.shape[1])
        scratch = scratch_of(z)
        chunks, span = z["NC"], z["CW"]
        anywhere = pl.BlockSpec(memory_space=pl.ANY)
        vmem = pl.BlockSpec(memory_space=pltpu.VMEM)
        operands = (
            row_plan,
            segments,
            norm_gain.reshape(1, width),
            queries,
            key_rows,
            value_rows,
            out_weight,
            out_grad,
        )
        kept = pl.pallas_call(
            functools.partial(whole_body, z, tuple(scratch)),
            out_shape=[
                pltpu.VMEM((chunks, rows, span), BF16),
                pltpu.VMEM((3, chunks, rows, span), BF16),
                pltpu.VMEM((chunks, z["RB"], span), F32),
            ],
            in_specs=[pl.BlockSpec(memory_space=pltpu.HBM)] * 8,
            out_specs=[vmem] * 3,
            scratch_shapes=list(scratch.values()),
            compiler_params=pltpu.CompilerParams(
                collective_id=0, has_side_effects=True, vmem_limit_bytes=50 * 1024 * 1024
            ),
        )(*(pltpu.with_memory_space_constraint(a, pltpu.HBM) for a in operands))
        half = jax.ShapeDtypeStruct((rows, width), BF16)
        return pl.pallas_call(
            functools.partial(write_body, z["HEADS"]),
            out_shape=[half, half, half, half, jax.ShapeDtypeStruct((z["RB"], width), F32)],
            in_specs=[anywhere] * 3,
            out_specs=[anywhere] * 5,
            scratch_shapes=[pltpu.SemaphoreType.DMA((chunks, 5))],
            compiler_params=pltpu.CompilerParams(vmem_limit_bytes=4 * 1024 * 1024),
        )(*kept)

    placed = (
        P(("dp", "seq"), "mp"),
        P(("dp", "seq"), "mp"),
        P(("dp", "seq"), "mp"),
        P(),
        P("dp", "seq"),
        P("mp"),
        P("mp", None),
        P(("dp", "seq"), "mp"),
    )
    return jax.shard_map(
        local, mesh=mesh, in_specs=placed, out_specs=(P(("dp", "seq"), "mp"),) * 5, check_vma=False
    )
```
